256 devices in a mesh: dp: 32 (over z_lo, x, core), tensor: 8 (over y, z_hi).
Axes of the slice: x: 4, y: 4, z: 8 (z_hi: 2, z_lo: 4; z = z_hi * 4 + z_lo), core: 2. Of those that a mesh axis runs over, the one named last changes fastest.
Arguments:
- hidden: bfloat16 [32768, 28672], P('dp', 'tensor'), may hold values from -6 to 6
- out_grad: bfloat16 [32768, 8192], P('dp', 'tensor'), may hold values from -6 to 6
- proj_in: bfloat16 [28672, 64], P('tensor'), may hold values from -0.03125 to 0.03125
- proj_out: bfloat16 [8192, 64], P('tensor'), may hold values from -0.0625 to 0.0625
- owner_ids: int32 [32768, 1], P('dp'), may hold values from 0 to 31; in each aligned block of 1024 rows (0 to 1023, 1024 to 2047, ...) at most 128 rows name the same one
- example_ids: int32 [32768], P('dp'), may hold values from 0 to 127
Outputs:
- kernel: float32 [4096, 4096], P('tensor', 'dp')
The draws below stay inside these ranges and needn't reach their ends.
Inputs may be any that keep to these rules, and one draw needn't show every extreme that they name: `owner_ids`: among the rows of one index of dp, at most 128 name the same owner, and every draw reaches 128.
All inputs are finite; a program needn't handle non-finite values.
Results may differ from the reference program's by a relative error of at most 0.009.
Values may be sent and summed in bfloat16 or wider, within the bound.
A program may use at most 64 MiB of HBM per device.

```python
import math
import jax
import jax.numpy as jnp
import numpy as np
from jax import lax

D = 8192
FF = 28672
R = 64
TOK_DEV = 1024
EX_DEV = 128
TOKENS = 32768
EXAMPLES = 4096
CAP = 128
N_DP = 32


def with_ends(array, stream_key, low, largest):
    index_at = [jax.random.randint(jax.random.fold_in(stream_key, axis), (), 0, length) for axis, length in enumerate(array.shape)]
    longest = array.shape.index(max(array.shape))
    beside = index_at[:longest] + [(index_at[longest] + 1) % array.shape[longest]] + index_at[longest + 1:]
    return array.at[tuple(index_at)].set(low).at[tuple(beside)].set(largest)


def block_levels(own_key, shape, cuts, least, largest):
    level, own = 1.0, jax.random.fold_in(own_key, 6)
    for position, blocks in cuts:
        draws = jnp.exp(jax.random.uniform(jax.random.fold_in(own, position), (blocks,), jnp.float32, least / len(cuts), largest / len(cuts)))
        level = level * jnp.repeat(draws, shape[position] // blocks).reshape([-1 if axis == position else 1 for axis in range(len(shape))])
    return level


def assign_block(stream_key, own, number, rows, amount, top, limit, slope):
    ranking = jax.random.permutation(stream_key, amount)
    packed, common = portions_of(amount, rows * top, limit, slope, True), portions_of(amount, rows * top, limit, slope, False)
    places = jnp.arange(amount)

    def named(lengths, rotation):
        used = int((lengths > 0).sum())
        fixed = max(1, used // 4)
        passed = fixed + (places - fixed + rotation * (used - fixed)) % max(1, amount - fixed)
        return jnp.zeros((amount,), jnp.int32).at[ranking[jnp.where(places < fixed, places, passed)]].set(jnp.asarray(lengths, jnp.int32))

    lengths = jnp.where(number % 4 == 0, named(packed, number // 4), named(common, number - number // 4 - 1))
    mixed = jax.random.permutation(jax.random.fold_in(own, 3), amount)
    giver, sink = mixed[0:amount // 2 * 2:2], mixed[1:amount // 2 * 2:2]
    room = jnp.minimum(lengths[giver] - 1, limit - lengths[sink]) // 2
    room = jnp.where((giver == ranking[0]) | (sink == ranking[0]) | (lengths[sink] == 0), 0, jnp.maximum(room, 0))
    passed = jax.random.randint(jax.random.fold_in(own, 4), (amount // 2,), 0, 1 << 20) % (room + 1)
    lengths = lengths.at[giver].add(-passed).at[sink].add(passed)
    members = jnp.searchsorted(jnp.cumsum(lengths), jnp.arange(rows * top), side="right").astype(jnp.int32)
    table = members.reshape(top, rows).T
    table = table[jax.random.permutation(jax.random.fold_in(own, 1), rows)]
    rotation = jax.random.randint(jax.random.fold_in(own, 2), (rows, 1), 0, top)
    return jnp.take_along_axis(table, (jnp.arange(top)[None, :] + rotation) % top, axis=1)


def portions_of(amount, total, reach, skew, full):
    portions = [(1 << 20) // math.isqrt(rank ** skew) + 1 for rank in range(1, amount + 1)]
    largest = reach if full else min(reach, max(-(-total // amount), total * portions[0] // sum(portions)))
    least = 1 if total - largest >= amount - 1 else 0
    given, surplus = [largest] + [least] * (amount - 1), total - largest - least * (amount - 1)
    while surplus > 0:
        free = [i for i in range(1, amount) if given[i] < largest] or [i for i in range(1, amount) if given[i] < reach]
        whole, left = sum([portions[i] for i in free]), surplus
        for i in free:
            more = min(reach - given[i], max(1, left * portions[i] // whole), surplus)
            given[i] = given[i] + more
            surplus = surplus - more
    return np.array(given)


def normal_values(key, dims, width, most, pieces=(), kind=jnp.bfloat16):
    gain = block_levels(key, dims, pieces, -0.22, 0.18) if pieces else 1.0
    drawn = jax.random.normal(key, dims, jnp.float32) * width * gain
    return jnp.minimum(jnp.maximum(drawn, -most), most).astype(kind)


def setup_inputs(seed: int = 0) -> dict:
    key_list = jax.random.split(jax.random.key(seed), 7)
    hidden = normal_values(key_list[0], (TOKENS, FF), 1.0, 6.0, ((0, 32), (1, 8)))
    out_grad = normal_values(key_list[1], (TOKENS, D), 1.0, 6.0, ((0, 32), (1, 8)))
    proj_in = normal_values(key_list[2], (FF, R), FF ** -0.5, 0.03125, ((0, 8),))
    proj_out = normal_values(key_list[3], (D, R), D ** -0.5, 0.0625, ((0, 8),))
    owner_ids_keys = jax.random.split(jax.random.fold_in(key_list[4], 1), TOKENS // TOK_DEV)
    owner_ids_turns = jax.random.permutation(jax.random.fold_in(key_list[4], 3), TOKENS // TOK_DEV)
    owner_ids = jax.vmap(lambda own, number: assign_block(jax.random.fold_in(key_list[4], 2), own, number, TOK_DEV, N_DP, 1, CAP, 2))(owner_ids_keys, owner_ids_turns).reshape((TOKENS, 1))
    example_ids = with_ends(jax.random.randint(key_list[5], (TOKENS,), 0, EX_DEV), jax.random.fold_in(key_list[5], 1), 0, EX_DEV - 1).astype(jnp.int32)
    return dict(hidden=hidden, out_grad=out_grad, proj_in=proj_in, proj_out=proj_out, owner_ids=owner_ids, example_ids=example_ids)


def reference(hidden, out_grad, proj_in, proj_out, owner_ids, example_ids):
    xproj = jnp.dot(hidden, proj_in, preferred_element_type=jnp.float32)
    gproj = jnp.dot(out_grad, proj_out, preferred_element_type=jnp.float32)
    example = (owner_ids[:, 0] * EX_DEV + example_ids).astype(jnp.int32)
    blocks = TOKENS // TOK_DEV
    xb = xproj.reshape(blocks, TOK_DEV, R)
    gb = gproj.reshape(blocks, TOK_DEV, R)
    ib = example.reshape(blocks, TOK_DEV)

    def accumulate(carry, inputs):
        xrows, grows, idrows = inputs
        outer = (xrows[:, :, None] * grows[:, None, :]).reshape(TOK_DEV, R * R)
        return carry + jax.ops.segment_sum(outer, idrows, num_segments=EXAMPLES), None

    start = jnp.zeros((EXAMPLES, R * R), jnp.float32)
    sums, unused = lax.scan(accumulate, start, (xb, gb, ib))
    counts = jax.ops.segment_sum(jnp.ones((TOKENS,), jnp.float32), example, num_segments=EXAMPLES)
    grads = (sums / jnp.maximum(counts, 1.0)[:, None]).astype(jnp.bfloat16)
    return jnp.dot(grads, grads.T, preferred_element_type=jnp.float32) / R
```

```python
import jax
import jax.numpy as jnp
from jax import lax
from jax.experimental import pallas as pl
from jax.experimental.pallas import tpu as pltpu
from jax.sharding import PartitionSpec as P

TOK = 1024
PART = 256
EX = 128
R = 64
HALF = 32
COLS = HALF * HALF
GROUP = 4
NT = (((1,), (1,)), ((), ()))
MESH = pl.DeviceIdType.MESH
BF = jnp.bfloat16
F32 = jnp.float32


def nt(a, b):
    return lax.dot_general(a, b, NT, preferred_element_type=F32)


def kernel(
    hid, og, pin, pout, own, exi, out,
    hbuf, gbuf, pinb, poutb, part_own, rs_send, rs_recv, z_send, z_recv, vals, slots,
    ids_send, ids_recv, sbuf, rbuf, outer, member, acc, bbuf, abuf, keep, c_send, c_recv,
    hsem, gsem, psem, rs_ss, rs_rs, z_sem, v_ss, v_rs, i_ss, i_rs, t_ss, t_rs,
    a_ss, a_rs, x_ss, x_rs, b_ss, b_rs, c_ss, c_rs,
):
    dp = lax.axis_index("dp")
    tn = lax.axis_index("tensor")
    y = tn // 2
    zh = lax.rem(tn, 2)
    zl = dp // 8
    x = lax.rem(dp // 2, 4)
    core = lax.rem(dp, 2)

    def remote(src, dst, ss, rs, **where):
        return pltpu.make_async_remote_copy(
            src_ref=src, dst_ref=dst, send_sem=ss, recv_sem=rs,
            device_id=where, device_id_type=MESH,
        )

    def at_y(k):
        return lax.rem(y + k, 4) * 2 + zh

    cp_in = pltpu.make_async_copy(pin, pinb, psem.at[0])
    cp_out = pltpu.make_async_copy(pout, poutb, psem.at[1])
    cp_out.start()
    cp_in.start()

    def load(k):
        p = lax.rem(y + 1 + k, 4)
        rows = pl.ds(pl.multiple_of(p * PART, PART), PART)
        return (
            pltpu.make_async_copy(og.at[rows], gbuf.at[p], gsem.at[k]),
            pltpu.make_async_copy(hid.at[rows], hbuf.at[p], hsem.at[k]),
        )

    for k in range(4):
        for cp in load(k):
            cp.start()

    barrier = pltpu.get_barrier_semaphore()

    def greet(k, c):
        pl.semaphore_signal(barrier, inc=1, device_id={"dp": lax.rem(dp + k, 32)}, device_id_type=MESH)
        return c

    lax.fori_loop(1, 32, greet, 0)
    for k in range(1, 4):
        pl.semaphore_signal(barrier, inc=1, device_id={"tensor": at_y(k)}, device_id_type=MESH)
    pl.semaphore_signal(barrier, inc=1, device_id={"tensor": y * 2 + 1 - zh}, device_id_type=MESH)

    hot = (own[...] - 8 * y == lax.broadcasted_iota(jnp.int32, (8, TOK), 0)).astype(F32)
    tri = (
        lax.broadcasted_iota(jnp.int32, (128, 128), 0) <= lax.broadcasted_iota(jnp.int32, (128, 128), 1)
    ).astype(BF)
    first = (lax.broadcasted_iota(jnp.int32, (8, 128), 0) * 128).astype(F32)
    carry = jnp.zeros((8, 1), F32)
    keys = []
    for b in range(8):
        h = hot[:, 128 * b : 128 * (b + 1)]
        rank = jnp.dot(h.astype(BF), tri, preferred_element_type=F32) + carry
        carry = carry + jnp.sum(h, 1, keepdims=True)
        keys.append(jnp.sum(h * (first + rank), 0, keepdims=True))
    key = jnp.concatenate(keys, 1).astype(jnp.int32) - 1
    idrow = jnp.broadcast_to((exi[...] + 1).astype(F32), (16, TOK)).astype(BF)
    for b in range(8):
        hit = key == lax.broadcasted_iota(jnp.int32, (128, TOK), 0) + 128 * b
        slots[128 * b : 128 * (b + 1), :] = hit.astype(F32).astype(BF)
        ids_send[b] = nt(idrow, slots[128 * b : 128 * (b + 1), :])[0:1, :]
    outer[COLS : COLS + 16, :] = jnp.ones((16, 128 * GROUP), BF)

    pl.semaphore_wait(barrier, 35)

    def ids_copy(k):
        dest = lax.rem(dp + k, 32)
        return remote(
            ids_send.at[lax.rem(dest, 8)], ids_recv.at[dp], i_ss.at[k], i_rs.at[dp], dp=dest
        )

    def ids_start(k, c):
        ids_copy(k).start()
        return c

    lax.fori_loop(1, 32, ids_start, 0)
    ids_recv[dp] = ids_send[lax.rem(dp, 8)]

    def rs_copy(k):
        p = lax.rem(y + 1 + k, 4)
        return remote(rs_send.at[k], rs_recv.at[y], rs_ss.at[k], rs_rs.at[y], tensor=p * 2 + zh)

    cp_out.wait()
    cp_in.wait()
    for k in range(4):
        p = lax.rem(y + 1 + k, 4)
        for cp in load(k):
            cp.wait()
        gp = nt(gbuf[p], poutb[...])
        xp = nt(hbuf[p], pinb[...])
        both = jnp.concatenate([xp, gp], 1).T
        if k < 3:
            rs_send[k] = both.astype(BF)
            rs_copy(k).start()
        else:
            part_own[...] = both

    total = part_own[...]
    for k in range(1, 4):
        src = lax.rem(y + k, 4)
        remote(
            rs_send.at[0], rs_recv.at[src], rs_ss.at[0], rs_rs.at[src], tensor=src * 2 + zh
        ).wait_recv()
        total = total + rs_recv[src].astype(F32)
    z_send[...] = total.astype(BF)
    z_copy = remote(z_send, z_recv, z_sem.at[0], z_sem.at[1], tensor=y * 2 + 1 - zh)
    z_copy.start()
    part_own[...] = total
    z_copy.wait_recv()
    vals[y] = (part_own[...] + z_recv[...].astype(F32)).astype(BF)

    def v_copy(k):
        return remote(vals.at[y], vals.at[y], v_ss.at[k], v_rs.at[y], tensor=at_y(k))

    for k in range(1, 4):
        v_copy(k).start()
    for k in range(1, 4):
        src = lax.rem(y + k, 4)
        remote(vals.at[src], vals.at[src], v_ss.at[k], v_rs.at[src], tensor=at_y(k)).wait_recv()

    for b in range(2):
        rows = slice(512 * b, 512 * (b + 1))
        routed = jnp.zeros((128, 512), F32)
        for p in range(4):
            routed = routed + nt(vals[p], slots[rows, PART * p : PART * (p + 1)])
        routed = routed.astype(BF)
        for o in range(4):
            piece = routed[:, 128 * o : 128 * (o + 1)]
            for s in range(4):
                sbuf[4 * b + o, s, 0:HALF, :] = piece[HALF * (s // 2) : HALF * (s // 2 + 1), :]
                sbuf[4 * b + o, s, HALF:R, :] = piece[R + HALF * (s % 2) : R + HALF * (s % 2 + 1), :]

    def tok_copy(k):
        dest = lax.rem(dp + k, 32)
        return remote(
            sbuf.at[lax.rem(dest, 8), dest // 8], rbuf.at[dp], t_ss.at[k], t_rs.at[dp], dp=dest
        )

    def tok_start(k, c):
        tok_copy(k).start()
        return c

    lax.fori_loop(1, 32, tok_start, 0)
    rbuf[dp] = sbuf[lax.rem(dp, 8), zl]
    acc[...] = jnp.zeros_like(acc)

    def kron(g, c):
        for s in range(GROUP):
            k = g * GROUP + s
            src = lax.rem(dp + 32 - k, 32)

            def arrived():
                remote(
                    ids_send.at[0], ids_recv.at[src], i_ss.at[0], i_rs.at[src], dp=src
                ).wait_recv()
                remote(
                    sbuf.at[0, 0], rbuf.at[src], t_ss.at[0], t_rs.at[src], dp=src
                ).wait_recv()

            if s == 0:
                pl.when(g > 0)(arrived)
            else:
                arrived()
            xr = rbuf[src, 0:HALF, :].astype(F32)
            gr = rbuf[src, HALF:R, :].astype(F32)
            lanes = slice(128 * s, 128 * (s + 1))
            for i in range(HALF):
                outer[HALF * i : HALF * (i + 1), lanes] = (xr[i : i + 1, :] * gr).astype(BF)
            ids = ids_recv[src].astype(jnp.int32)
            member[:, lanes] = (
                (ids == lax.broadcasted_iota(jnp.int32, (EX, 128), 0) + 1).astype(F32).astype(BF)
            )
        acc[...] += nt(outer[...], member[...])
        return c

    lax.fori_loop(0, 32 // GROUP, kron, 0)

    scale = 1.0 / jnp.maximum(acc[COLS : COLS + 1, :], 1.0)
    for b in range(COLS // 128):
        rows = slice(128 * b, 128 * (b + 1))
        bbuf[y, :, rows] = (acc[rows, :] * scale).T.astype(BF)

    yp, ym = at_y(1), at_y(3)
    low, high = pl.ds(0, 64), pl.ds(64, 64)
    before, after, across = lax.rem(y + 3, 4), lax.rem(y + 1, 4), lax.rem(y + 2, 4)
    r = lax.rem(x + 4 - 2 * zh, 4)
    mine = jnp.where(r < 2, r, 3 - r)
    other = 1 - mine

    def at_x(k):
        return zl * 8 + lax.rem(x + k, 4) * 2 + core

    b_up = remote(bbuf.at[y], bbuf.at[y], b_ss.at[0], b_rs.at[0], tensor=yp)
    b_down = remote(bbuf.at[y], bbuf.at[y], b_ss.at[1], b_rs.at[1], tensor=ym)
    b_up.start()
    b_down.start()

    def a_first(h, side):
        rows = pl.ds(64 * h, 64)
        return remote(
            bbuf.at[y, rows], abuf.at[mine * 2 + core, rows], a_ss.at[side, h], a_rs.at[mine, h],
            dp=at_x(1 if side == 0 else 3),
        )

    def a_next(h):
        rows = pl.ds(64 * h, 64)
        slot = abuf.at[mine * 2 + core, rows]
        return remote(
            slot, slot, a_ss.at[0, h], a_rs.at[mine, h], dp=at_x(1 + 2 * (r - 2))
        )

    def a_wait(which, h):
        slot = abuf.at[which * 2 + core, pl.ds(64 * h, 64)]
        remote(slot, slot, a_ss.at[0, h], a_rs.at[which, h], dp=at_x(1)).wait_recv()

    @pl.when(r < 2)
    def _():
        for h in range(2):
            a_first(h, 0).start()
            a_first(h, 1).start()
        abuf[mine * 2 + core] = bbuf[y]

    @pl.when(r >= 2)
    def _():
        for h in range(2):
            a_wait(mine, h)
            a_next(h).start()

    twin = dp + 1 - 2 * core

    def x_copy(which):
        slot = abuf.at[which * 2 + core]
        return remote(slot, slot, x_ss.at[which], x_rs.at[which], dp=twin)

    x_copy(mine).start()

    remote(bbuf.at[before], bbuf.at[before], b_ss.at[0], b_rs.at[0], tensor=ym).wait_recv()
    b_fwd_up = remote(bbuf.at[before, low], bbuf.at[before, low], b_ss.at[2], b_rs.at[2], tensor=yp)
    b_fwd_up.start()
    remote(bbuf.at[after], bbuf.at[after], b_ss.at[1], b_rs.at[1], tensor=yp).wait_recv()
    b_fwd_down = remote(bbuf.at[after, high], bbuf.at[after, high], b_ss.at[3], b_rs.at[3], tensor=ym)
    b_fwd_down.start()

    for h in range(2):
        a_wait(other, h)
    x_copy(other).start()
    for which in range(2):
        slot = abuf.at[which * 2 + 1 - core]
        remote(slot, slot, x_ss.at[which], x_rs.at[which], dp=twin).wait_recv()

    rows_a = abuf[...].reshape(4 * EX, COLS)

    def c_copy(q):
        return remote(c_send.at[q], c_recv.at[zl], c_ss.at[q], c_rs.at[zl], dp=q * 8 + x * 2 + core)

    for k in (0, 1, 3, 2):
        q = lax.rem(y + k, 4)
        if k == 2:
            remote(
                bbuf.at[across, low], bbuf.at[across, low], b_ss.at[2], b_rs.at[2], tensor=ym
            ).wait_recv()
            remote(
                bbuf.at[across, high], bbuf.at[across, high], b_ss.at[3], b_rs.at[3], tensor=yp
            ).wait_recv()
        block = nt(rows_a, bbuf[q]) * (1.0 / R)

        @pl.when(q == zl)
        def _():
            keep[...] = block

        @pl.when(q != zl)
        def _():
            c_send[q] = block.astype(BF)
            c_copy(q).start()

    result = keep[...]
    for k in range(1, 4):
        src = lax.rem(zl + k, 4)
        remote(c_send.at[src], c_recv.at[src], c_ss.at[src], c_rs.at[src], dp=src * 8 + x * 2 + core).wait_recv()
        result = result + c_recv[src].astype(F32)
    out[...] = result

    def left(k, c):
        ids_copy(k).wait_send()
        tok_copy(k).wait_send()
        return c

    lax.fori_loop(1, 32, left, 0)
    for k in range(3):
        rs_copy(k).wait_send()
        v_copy(k + 1).wait_send()
        c_copy(lax.rem(zl + k + 1, 4)).wait_send()
    z_copy.wait_send()
    for cp in (b_up, b_down, b_fwd_up, b_fwd_down, x_copy(0), x_copy(1)):
        cp.wait_send()

    @pl.when(r < 2)
    def _():
        for h in range(2):
            a_first(h, 0).wait_send()
            a_first(h, 1).wait_send()

    @pl.when(r >= 2)
    def _():
        for h in range(2):
            a_next(h).wait_send()


def body(hidden, out_grad, proj_in, proj_out, owner_ids, example_ids):
    wide, model = hidden.shape[1], out_grad.shape[1]
    hbm = pl.BlockSpec(memory_space=pltpu.HBM)
    vmem = pl.BlockSpec(memory_space=pltpu.VMEM)
    dma = pltpu.SemaphoreType.DMA
    return pl.pallas_call(
        kernel,
        out_shape=jax.ShapeDtypeStruct((4 * EX, EX), F32),
        in_specs=[hbm, hbm, hbm, hbm, vmem, vmem],
        out_specs=vmem,
        scratch_shapes=[
            pltpu.VMEM((4, PART, wide), BF),
            pltpu.VMEM((4, PART, model), BF),
            pltpu.VMEM((R, wide), BF),
            pltpu.VMEM((R, model), BF),
            pltpu.VMEM((2 * R, PART), F32),
            pltpu.VMEM((3, 2 * R, PART), BF),
            pltpu.VMEM((4, 2 * R, PART), BF),
            pltpu.VMEM((2 * R, PART), BF),
            pltpu.VMEM((2 * R, PART), BF),
            pltpu.VMEM((4, 2 * R, PART), BF),
            pltpu.VMEM((8 * 128, TOK), BF),
            pltpu.VMEM((8, 1, 128), F32),
            pltpu.VMEM((32, 1, 128), F32),
            pltpu.VMEM((8, 4, R, 128), BF),
            pltpu.VMEM((32, R, 128), BF),
            pltpu.VMEM((COLS + 16, 128 * GROUP), BF),
            pltpu.VMEM((EX, 128 * GROUP), BF),
            pltpu.VMEM((COLS + 16, EX), F32),
            pltpu.VMEM((4, EX, COLS), BF),
            pltpu.VMEM((4, EX, COLS), BF),
            pltpu.VMEM((4 * EX, EX), F32),
            pltpu.VMEM((4, 4 * EX, EX), BF),
            pltpu.VMEM((4, 4 * EX, EX), BF),
            dma((4,)), dma((4,)), dma((2,)), dma((3,)), dma((4,)), dma((2,)), dma((4,)), dma((4,)),
            dma((32,)), dma((32,)), dma((32,)), dma((32,)),
            dma((2, 2)), dma((2, 2)), dma((2,)), dma((2,)), dma((4,)), dma((4,)), dma((4,)), dma((4,)),
        ],
        compiler_params=pltpu.CompilerParams(
            collective_id=0, has_side_effects=True, vmem_limit_bytes=48 * 1024 * 1024
        ),
        name="per_example_kernel",
    )(hidden, out_grad, proj_in.T, proj_out.T, owner_ids.reshape(1, TOK), example_ids.reshape(1, TOK))


def solution(mesh):
    in_specs = (
        P("dp", "tensor"),
        P("dp", "tensor"),
        P("tensor", None),
        P("tensor", None),
        P("dp", None),
        P("dp"),
    )
    out_specs = P("tensor", "dp")
    return jax.shard_map(body, mesh=mesh, in_specs=in_specs, out_specs=out_specs, check_vma=False)
```

```python
import jax
import jax.numpy as jnp
from jax import lax
from jax.experimental import pallas as pl
from jax.experimental.pallas import tpu as pltpu
from jax.sharding import PartitionSpec as P

TOK = 1024
PART = 256
EX = 128
R = 64
HALF = 32
COLS = HALF * HALF
GROUP = 4
NT = (((1,), (1,)), ((), ()))
MESH = pl.DeviceIdType.MESH
BF = jnp.bfloat16
F32 = jnp.float32


def nt(a, b):
    return lax.dot_general(a, b, NT, preferred_element_type=F32)


def kernel(
    hid, og, pin, pout, own_in, exi_in, out,
    own, exi,
    hbuf, gbuf, pinb, poutb, part_own, rs_send, rs_recv, z_send, z_recv, vals, slots,
    routed, sbuf, rbuf, outer, member, acc, bbuf, abuf, keep, c_send, c_recv,
    hsem, gsem, psem, rs_ss, rs_rs, z_ss, z_rs, v_ss, v_rs, t_ss, t_rs,
    a_ss, a_rs, x_ss, x_rs, b_ss, b_rs, c_ss, c_rs,
):
    dp = lax.axis_index("dp")
    tn = lax.axis_index("tensor")
    y = tn // 2
    zh = lax.rem(tn, 2)
    zl = dp // 8
    x = lax.rem(dp // 2, 4)
    core = lax.rem(dp, 2)

    def remote(src, dst, ss, rs, **where):
        return pltpu.make_async_remote_copy(
            src_ref=src, dst_ref=dst, send_sem=ss, recv_sem=rs,
            device_id=where, device_id_type=MESH,
        )

    def at_y(k):
        return lax.rem(y + k, 4) * 2 + zh

    cp_in = pltpu.make_async_copy(pin, pinb, psem.at[0])
    cp_out = pltpu.make_async_copy(pout, poutb, psem.at[1])
    cp_own = pltpu.make_async_copy(own_in, own, psem.at[2])
    cp_exi = pltpu.make_async_copy(exi_in, exi, psem.at[3])
    cp_own.start()
    cp_exi.start()
    cp_out.start()
    cp_in.start()

    def load(k):
        p = lax.rem(y + 1 + k, 4)
        rows = pl.ds(pl.multiple_of(p * PART, PART), PART)
        return (
            pltpu.make_async_copy(og.at[rows], gbuf.at[p], gsem.at[k]),
            pltpu.make_async_copy(hid.at[rows], hbuf.at[p], hsem.at[k]),
        )

    for k in range(4):
        for cp in load(k):
            cp.start()

    barrier = pltpu.get_barrier_semaphore()

    def greet(k, c):
        pl.semaphore_signal(barrier, inc=1, device_id={"dp": lax.rem(dp + k, 32)}, device_id_type=MESH)
        return c

    lax.fori_loop(1, 32, greet, 0)
    for k in range(1, 4):
        pl.semaphore_signal(barrier, inc=1, device_id={"tensor": at_y(k)}, device_id_type=MESH)
    pl.semaphore_signal(barrier, inc=1, device_id={"tensor": y * 2 + 1 - zh}, device_id_type=MESH)

    cp_own.wait()
    cp_exi.wait()
    hot = (own[...] - 8 * y == lax.broadcasted_iota(jnp.int32, (8, TOK), 0)).astype(F32)
    tri = (
        lax.broadcasted_iota(jnp.int32, (128, 128), 0) <= lax.broadcasted_iota(jnp.int32, (128, 128), 1)
    ).astype(BF)
    first = (lax.broadcasted_iota(jnp.int32, (8, 128), 0) * 128).astype(F32)
    carry = jnp.zeros((8, 1), F32)
    keys = []
    for b in range(8):
        h = hot[:, 128 * b : 128 * (b + 1)]
        rank = jnp.dot(h.astype(BF), tri, preferred_element_type=F32) + carry
        carry = carry + jnp.sum(h, 1, keepdims=True)
        keys.append(jnp.sum(h * (first + rank), 0, keepdims=True))
    order = [2 * p + ch for ch in range(2) for p in range(4)]
    key = jnp.concatenate([keys[b] for b in order], 1).astype(jnp.int32) - 1
    idrow = (exi[...] + 1).astype(F32)
    idrow = jnp.concatenate([idrow[:, 128 * b : 128 * (b + 1)] for b in order], 1)
    idrow = jnp.broadcast_to(idrow, (16, TOK)).astype(BF)
    for o in range(8):
        hit = key == lax.broadcasted_iota(jnp.int32, (128, TOK), 0) + 128 * o
        slots[128 * o : 128 * (o + 1), :] = hit.astype(F32).astype(BF)
        ids = nt(idrow, slots[128 * o : 128 * (o + 1), :])[0:8, :].astype(BF)
        for q in range(4):
            sbuf[o, q, R : R + 8, :] = ids
    outer[COLS : COLS + 16, :] = jnp.ones((16, 128 * GROUP), BF)
    acc[...] = jnp.zeros_like(acc)

    def rs_copy(k):
        p = lax.rem(y + 1 + k, 4)
        return remote(rs_send.at[k], rs_recv.at[y], rs_ss.at[k], rs_rs.at[y], tensor=p * 2 + zh)

    def project(k):
        p = lax.rem(y + 1 + k, 4)
        for cp in load(k):
            cp.wait()
        gp = nt(gbuf[p], poutb[...])
        xp = nt(hbuf[p], pinb[...])
        return jnp.concatenate([xp, gp], 1).T

    cp_out.wait()
    cp_in.wait()
    for k in range(3):
        both = project(k).astype(BF)
        rs_send[k, 0] = both[:, :128]
        rs_send[k, 1] = both[:, 128:]
    pl.semaphore_wait(barrier, 35)
    for k in range(3):
        rs_copy(k).start()
    both = project(3)
    part_own[0] = both[:, :128]
    part_own[1] = both[:, 128:]

    for k in range(1, 4):
        src = lax.rem(y + k, 4)
        remote(
            rs_send.at[0], rs_recv.at[src], rs_ss.at[0], rs_rs.at[src], tensor=src * 2 + zh
        ).wait_recv()

    def z_copy(ch):
        return remote(z_send.at[ch], z_recv.at[ch], z_ss.at[ch], z_rs.at[ch], tensor=y * 2 + 1 - zh)

    for ch in range(2):
        total = part_own[ch]
        for k in range(1, 4):
            total = total + rs_recv[lax.rem(y + k, 4), ch].astype(F32)
        z_send[ch] = total.astype(BF)
        z_copy(ch).start()
        part_own[ch] = total

    def v_copy(ch, k):
        return remote(vals.at[ch, y], vals.at[ch, y], v_ss.at[ch, k], v_rs.at[ch, y], tensor=at_y(k))

    for ch in range(2):
        z_copy(ch).wait_recv()
        vals[ch, y] = (part_own[ch] + z_recv[ch].astype(F32)).astype(BF)
        for k in range(1, 4):
            v_copy(ch, k).start()

    for ch in range(2):
        for k in range(1, 4):
            src = lax.rem(y + k, 4)
            remote(
                vals.at[ch, src], vals.at[ch, src], v_ss.at[ch, k], v_rs.at[ch, src], tensor=at_y(k)
            ).wait_recv()
        part = jnp.concatenate([vals[ch, p] for p in range(4)], 1)
        for b in range(2):
            rows = slice(512 * b, 512 * (b + 1))
            placed = nt(part, slots[rows, 512 * ch : 512 * (ch + 1)])
            if ch == 0:
                routed[:, rows] = placed
                continue
            placed = (placed + routed[:, rows]).astype(BF)
            for o in range(4):
                piece = placed[:, 128 * o : 128 * (o + 1)]
                for q in range(4):
                    sbuf[4 * b + o, q, 0:HALF, :] = piece[HALF * (q // 2) : HALF * (q // 2 + 1), :]
                    sbuf[4 * b + o, q, HALF:R, :] = piece[R + HALF * (q % 2) : R + HALF * (q % 2 + 1), :]

    def tok_copy(k):
        dest = lax.rem(dp + k, 32)
        return remote(
            sbuf.at[lax.rem(dest, 8), dest // 8], rbuf.at[dp], t_ss.at[k], t_rs.at[dp], dp=dest
        )

    def tok_start(k, c):
        tok_copy(k).start()
        return c

    lax.fori_loop(1, 32, tok_start, 0)
    rbuf[dp] = sbuf[lax.rem(dp, 8), zl]

    def kron(g, c):
        for s in range(GROUP):
            k = g * GROUP + s
            src = lax.rem(dp + 32 - k, 32)

            def arrived():
                remote(
                    sbuf.at[0, 0], rbuf.at[src], t_ss.at[0], t_rs.at[src], dp=src
                ).wait_recv()

            if s == 0:
                pl.when(g > 0)(arrived)
            else:
                arrived()
            xr = rbuf[src, 0:HALF, :].astype(F32)
            gr = rbuf[src, HALF:R, :].astype(F32)
            lanes = slice(128 * s, 128 * (s + 1))
            for i in range(HALF):
                outer[HALF * i : HALF * (i + 1), lanes] = (xr[i : i + 1, :] * gr).astype(BF)
            ids = rbuf[src, R : R + 8, :].astype(F32)[0:1, :].astype(jnp.int32)
            member[:, lanes] = (
                (ids == lax.broadcasted_iota(jnp.int32, (EX, 128), 0) + 1).astype(F32).astype(BF)
            )
        acc[...] += nt(outer[...], member[...])
        return c

    lax.fori_loop(0, 32 // GROUP, kron, 0)

    scale = 1.0 / jnp.maximum(acc[COLS : COLS + 1, :], 1.0)
    for b in range(COLS // 128):
        rows = slice(128 * b, 128 * (b + 1))
        bbuf[y, :, rows] = (acc[rows, :] * scale).T.astype(BF)

    yp, ym = at_y(1), at_y(3)
    low, high = pl.ds(0, 64), pl.ds(64, 64)
    before, after, across = lax.rem(y + 3, 4), lax.rem(y + 1, 4), lax.rem(y + 2, 4)
    r = lax.rem(x + 4 - 2 * zh, 4)
    mine = jnp.where(r < 2, r, 3 - r)
    other = 1 - mine

    def at_x(k):
        return zl * 8 + lax.rem(x + k, 4) * 2 + core

    b_up = remote(bbuf.at[y], bbuf.at[y], b_ss.at[0], b_rs.at[0], tensor=yp)
    b_down = remote(bbuf.at[y], bbuf.at[y], b_ss.at[1], b_rs.at[1], tensor=ym)
    b_up.start()
    b_down.start()

    def a_first(h, side):
        rows = pl.ds(64 * h, 64)
        return remote(
            bbuf.at[y, rows], abuf.at[mine * 2 + core, rows], a_ss.at[side, h], a_rs.at[mine, h],
            dp=at_x(1 if side == 0 else 3),
        )

    def a_next(h):
        rows = pl.ds(64 * h, 64)
        slot = abuf.at[mine * 2 + core, rows]
        return remote(
            slot, slot, a_ss.at[0, h], a_rs.at[mine, h], dp=at_x(1 + 2 * (r - 2))
        )

    def a_wait(which, h):
        slot = abuf.at[which * 2 + core, pl.ds(64 * h, 64)]
        remote(slot, slot, a_ss.at[0, h], a_rs.at[which, h], dp=at_x(1)).wait_recv()

    @pl.when(r < 2)
    def _():
        for h in range(2):
            a_first(h, 0).start()
            a_first(h, 1).start()
        abuf[mine * 2 + core] = bbuf[y]

    @pl.when(r >= 2)
    def _():
        for h in range(2):
            a_wait(mine, h)
            a_next(h).start()

    twin = dp + 1 - 2 * core

    def x_copy(which):
        slot = abuf.at[which * 2 + core]
        return remote(slot, slot, x_ss.at[which], x_rs.at[which], dp=twin)

    def x_wait(which):
        slot = abuf.at[which * 2 + 1 - core]
        remote(slot, slot, x_ss.at[which], x_rs.at[which], dp=twin).wait_recv()

    def c_copy(q, which):
        rows = pl.ds(pl.multiple_of(2 * EX * which, 2 * EX), 2 * EX)
        return remote(
            c_send.at[q, rows], c_recv.at[zl, rows], c_ss.at[q, which], c_rs.at[zl, which],
            dp=q * 8 + x * 2 + core,
        )

    def block(which, q):
        rows = pl.ds(pl.multiple_of(2 * EX * which, 2 * EX), 2 * EX)
        a = abuf[pl.ds(which * 2, 2)].reshape(2 * EX, COLS)
        product = nt(a, bbuf[q]) * (1.0 / R)

        @pl.when(q == zl)
        def _():
            keep[rows, :] = product

        @pl.when(q != zl)
        def _():
            c_send[q, rows, :] = product.astype(BF)
            c_copy(q, which).start()

    x_copy(mine).start()
    x_wait(mine)
    block(mine, y)
    remote(bbuf.at[before], bbuf.at[before], b_ss.at[0], b_rs.at[0], tensor=ym).wait_recv()
    b_fwd_up = remote(bbuf.at[before, low], bbuf.at[before, low], b_ss.at[2], b_rs.at[2], tensor=yp)
    b_fwd_up.start()
    remote(bbuf.at[after], bbuf.at[after], b_ss.at[1], b_rs.at[1], tensor=yp).wait_recv()
    b_fwd_down = remote(bbuf.at[after, high], bbuf.at[after, high], b_ss.at[3], b_rs.at[3], tensor=ym)
    b_fwd_down.start()
    block(mine, after)
    block(mine, before)
    for h in range(2):
        a_wait(other, h)
    x_copy(other).start()
    x_wait(other)
    block(other, y)
    block(other, after)
    block(other, before)
    remote(bbuf.at[across, low], bbuf.at[across, low], b_ss.at[2], b_rs.at[2], tensor=ym).wait_recv()
    remote(bbuf.at[across, high], bbuf.at[across, high], b_ss.at[3], b_rs.at[3], tensor=yp).wait_recv()
    block(mine, across)
    block(other, across)

    result = keep[...]
    for k in range(1, 4):
        src = lax.rem(zl + k, 4)
        for which in range(2):
            rows = slice(2 * EX * which, 2 * EX * (which + 1))
            remote(
                c_send.at[src, rows], c_recv.at[src, rows], c_ss.at[src, which], c_rs.at[src, which],
                dp=src * 8 + x * 2 + core,
            ).wait_recv()
        result = result + c_recv[src].astype(F32)
    out[...] = result

    def left(k, c):
        tok_copy(k).wait_send()
        return c

    lax.fori_loop(1, 32, left, 0)
    for k in range(3):
        rs_copy(k).wait_send()
        for h in range(2):
            v_copy(h, k + 1).wait_send()
            c_copy(lax.rem(zl + k + 1, 4), h).wait_send()
    for h in range(2):
        z_copy(h).wait_send()
    for cp in (b_up, b_down, b_fwd_up, b_fwd_down, x_copy(0), x_copy(1)):
        cp.wait_send()

    @pl.when(r < 2)
    def _():
        for h in range(2):
            a_first(h, 0).wait_send()
            a_first(h, 1).wait_send()

    @pl.when(r >= 2)
    def _():
        for h in range(2):
            a_next(h).wait_send()


def body(hidden, out_grad, proj_in, proj_out, owner_ids, example_ids):
    wide, model = hidden.shape[1], out_grad.shape[1]
    hbm = pl.BlockSpec(memory_space=pltpu.HBM)
    vmem = pl.BlockSpec(memory_space=pltpu.VMEM)
    dma = pltpu.SemaphoreType.DMA
    return pl.pallas_call(
        kernel,
        out_shape=jax.ShapeDtypeStruct((4 * EX, EX), F32),
        in_specs=[hbm] * 6,
        out_specs=vmem,
        scratch_shapes=[
            pltpu.VMEM((1, TOK), jnp.int32),
            pltpu.VMEM((1, TOK), jnp.int32),
            pltpu.VMEM((4, PART, wide), BF),
            pltpu.VMEM((4, PART, model), BF),
            pltpu.VMEM((R, wide), BF),
            pltpu.VMEM((R, model), BF),
            pltpu.VMEM((2, 2 * R, 128), F32),
            pltpu.VMEM((3, 2, 2 * R, 128), BF),
            pltpu.VMEM((4, 2, 2 * R, 128), BF),
            pltpu.VMEM((2, 2 * R, 128), BF),
            pltpu.VMEM((2, 2 * R, 128), BF),
            pltpu.VMEM((2, 4, 2 * R, 128), BF),
            pltpu.VMEM((8 * 128, TOK), BF),
            pltpu.VMEM((2 * R, 8 * 128), F32),
            pltpu.VMEM((8, 4, R + 8, 128), BF),
            pltpu.VMEM((32, R + 8, 128), BF),
            pltpu.VMEM((COLS + 16, 128 * GROUP), BF),
            pltpu.VMEM((EX, 128 * GROUP), BF),
            pltpu.VMEM((COLS + 16, EX), F32),
            pltpu.VMEM((4, EX, COLS), BF),
            pltpu.VMEM((4, EX, COLS), BF),
            pltpu.VMEM((4 * EX, EX), F32),
            pltpu.VMEM((4, 4 * EX, EX), BF),
            pltpu.VMEM((4, 4 * EX, EX), BF),
            dma((4,)), dma((4,)), dma((4,)), dma((3,)), dma((4,)), dma((2,)), dma((2,)),
            dma((2, 4)), dma((2, 4)), dma((32,)), dma((32,)),
            dma((2, 2)), dma((2, 2)), dma((2,)), dma((2,)), dma((4,)), dma((4,)), dma((4, 2)), dma((4, 2)),
        ],
        compiler_params=pltpu.CompilerParams(
            collective_id=0, has_side_effects=True, vmem_limit_bytes=60 * 1024 * 1024
        ),
        name="per_example_kernel",
    )(hidden, out_grad, proj_in.T, proj_out.T, owner_ids.reshape(1, TOK), example_ids.reshape(1, TOK))


def solution(mesh):
    in_specs = (
        P("dp", "tensor"),
        P("dp", "tensor"),
        P("tensor", None),
        P("tensor", None),
        P("dp", None),
        P("dp"),
    )
    out_specs = P("tensor", "dp")
    return jax.shard_map(body, mesh=mesh, in_specs=in_specs, out_specs=out_specs, check_vma=False)
```

```python
import jax
import jax.numpy as jnp
from jax import lax
from jax.experimental import pallas as pl
from jax.experimental.pallas import tpu as pltpu
from jax.sharding import PartitionSpec as P

TOK = 1024
PART = 256
EX = 128
R = 64
HALF = 32
COLS = HALF * HALF
GROUP = 4
CHUNKS = 4
WIDE = COLS // CHUNKS
NT = (((1,), (1,)), ((), ()))
MESH = pl.DeviceIdType.MESH
BF = jnp.bfloat16
F32 = jnp.float32


def nt(a, b):
    return lax.dot_general(a, b, NT, preferred_element_type=F32)


def kernel(
    hid, og, pin, pout, own_in, exi_in, out,
    own, exi,
    hbuf, gbuf, pinb, poutb, part_own, rs_send, rs_recv, z_send, z_recv, vals, slots,
    routed, sbuf, rbuf, outer, member, acc, bbuf, abuf, keep, c_send, c_recv,
    hsem, gsem, psem, rs_ss, rs_rs, z_ss, z_rs, v_ss, v_rs, t_ss, t_rs,
    a_ss, a_rs, x_ss, x_rs, b_ss, b_rs, c_ss, c_rs,
):
    dp = lax.axis_index("dp")
    tn = lax.axis_index("tensor")
    y = tn // 2
    zh = lax.rem(tn, 2)
    zl = dp // 8
    x = lax.rem(dp // 2, 4)
    core = lax.rem(dp, 2)

    def remote(src, dst, ss, rs, **where):
        return pltpu.make_async_remote_copy(
            src_ref=src, dst_ref=dst, send_sem=ss, recv_sem=rs,
            device_id=where, device_id_type=MESH,
        )

    def at_y(k):
        return lax.rem(y + k, 4) * 2 + zh

    cp_in = pltpu.make_async_copy(pin, pinb, psem.at[0])
    cp_out = pltpu.make_async_copy(pout, poutb, psem.at[1])
    cp_own = pltpu.make_async_copy(own_in, own, psem.at[2])
    cp_exi = pltpu.make_async_copy(exi_in, exi, psem.at[3])
    cp_own.start()
    cp_exi.start()
    cp_out.start()
    cp_in.start()

    def load(k):
        p = lax.rem(y + 1 + k, 4)
        rows = pl.ds(pl.multiple_of(p * PART, PART), PART)
        return (
            pltpu.make_async_copy(og.at[rows], gbuf.at[p], gsem.at[k]),
            pltpu.make_async_copy(hid.at[rows], hbuf.at[p], hsem.at[k]),
        )

    for k in range(4):
        for cp in load(k):
            cp.start()

    barrier = pltpu.get_barrier_semaphore()

    def greet(k, c):
        pl.semaphore_signal(barrier, inc=1, device_id={"dp": lax.rem(dp + k, 32)}, device_id_type=MESH)
        return c

    lax.fori_loop(1, 32, greet, 0)
    for k in range(1, 4):
        pl.semaphore_signal(barrier, inc=1, device_id={"tensor": at_y(k)}, device_id_type=MESH)
    pl.semaphore_signal(barrier, inc=1, device_id={"tensor": y * 2 + 1 - zh}, device_id_type=MESH)

    cp_own.wait()
    cp_exi.wait()
    hot = (own[...] - 8 * y == lax.broadcasted_iota(jnp.int32, (8, TOK), 0)).astype(F32)
    tri = (
        lax.broadcasted_iota(jnp.int32, (128, 128), 0) <= lax.broadcasted_iota(jnp.int32, (128, 128), 1)
    ).astype(BF)
    first = (lax.broadcasted_iota(jnp.int32, (8, 128), 0) * 128).astype(F32)
    carry = jnp.zeros((8, 1), F32)
    keys = []
    for b in range(8):
        h = hot[:, 128 * b : 128 * (b + 1)]
        rank = jnp.dot(h.astype(BF), tri, preferred_element_type=F32) + carry
        carry = carry + jnp.sum(h, 1, keepdims=True)
        keys.append(jnp.sum(h * (first + rank), 0, keepdims=True))
    order = [2 * p + ch for ch in range(2) for p in range(4)]
    key = jnp.concatenate([keys[b] for b in order], 1).astype(jnp.int32) - 1
    idrow = (exi[...] + 1).astype(F32)
    idrow = jnp.concatenate([idrow[:, 128 * b : 128 * (b + 1)] for b in order], 1)
    idrow = jnp.broadcast_to(idrow, (16, TOK)).astype(BF)
    for o in range(8):
        hit = key == lax.broadcasted_iota(jnp.int32, (128, TOK), 0) + 128 * o
        slots[128 * o : 128 * (o + 1), :] = hit.astype(F32).astype(BF)
        ids = nt(idrow, slots[128 * o : 128 * (o + 1), :])[0:8, :].astype(BF)
        for q in range(4):
            sbuf[o, q, R : R + 8, :] = ids
    outer[COLS : COLS + 16, :] = jnp.ones((16, 128 * GROUP), BF)
    acc[...] = jnp.zeros_like(acc)

    def rs_copy(k):
        p = lax.rem(y + 1 + k, 4)
        return remote(rs_send.at[k], rs_recv.at[y], rs_ss.at[k], rs_rs.at[y], tensor=p * 2 + zh)

    def project(k):
        p = lax.rem(y + 1 + k, 4)
        for cp in load(k):
            cp.wait()
        gp = nt(gbuf[p], poutb[...])
        xp = nt(hbuf[p], pinb[...])
        return jnp.concatenate([xp, gp], 1).T

    cp_out.wait()
    cp_in.wait()
    for k in range(3):
        both = project(k).astype(BF)
        rs_send[k, 0] = both[:, :128]
        rs_send[k, 1] = both[:, 128:]
        if k == 0:
            pl.semaphore_wait(barrier, 35)
        rs_copy(k).start()
    both = project(3)
    part_own[0] = both[:, :128]
    part_own[1] = both[:, 128:]

    for k in range(1, 4):
        src = lax.rem(y + k, 4)
        remote(
            rs_send.at[0], rs_recv.at[src], rs_ss.at[0], rs_rs.at[src], tensor=src * 2 + zh
        ).wait_recv()

    def z_copy(ch):
        return remote(z_send.at[ch], z_recv.at[ch], z_ss.at[ch], z_rs.at[ch], tensor=y * 2 + 1 - zh)

    for ch in range(2):
        total = part_own[ch]
        for k in range(1, 4):
            total = total + rs_recv[lax.rem(y + k, 4), ch].astype(F32)
        z_send[ch] = total.astype(BF)
        z_copy(ch).start()
        part_own[ch] = total

    def v_copy(ch, k):
        return remote(vals.at[ch, y], vals.at[ch, y], v_ss.at[ch, k], v_rs.at[ch, y], tensor=at_y(k))

    for ch in range(2):
        z_copy(ch).wait_recv()
        vals[ch, y] = (part_own[ch] + z_recv[ch].astype(F32)).astype(BF)
        for k in range(1, 4):
            v_copy(ch, k).start()

    for ch in range(2):
        for k in range(1, 4):
            src = lax.rem(y + k, 4)
            remote(
                vals.at[ch, src], vals.at[ch, src], v_ss.at[ch, k], v_rs.at[ch, src], tensor=at_y(k)
            ).wait_recv()
        part = jnp.concatenate([vals[ch, p] for p in range(4)], 1)
        for b in range(2):
            rows = slice(512 * b, 512 * (b + 1))
            placed = nt(part, slots[rows, 512 * ch : 512 * (ch + 1)])
            if ch == 0:
                routed[:, rows] = placed
                continue
            placed = (placed + routed[:, rows]).astype(BF)
            for o in range(4):
                piece = placed[:, 128 * o : 128 * (o + 1)]
                for q in range(4):
                    sbuf[4 * b + o, q, 0:HALF, :] = piece[HALF * (q // 2) : HALF * (q // 2 + 1), :]
                    sbuf[4 * b + o, q, HALF:R, :] = piece[R + HALF * (q % 2) : R + HALF * (q % 2 + 1), :]

    xc = lax.rem(dp, 8)

    def tok_copy(dz, j):
        zq, xq = lax.rem(zl + dz, 4), lax.rem(xc + j, 8)
        return remote(
            sbuf.at[xq, zq], rbuf.at[dp], t_ss.at[dz * 8 + j], t_rs.at[dp], dp=zq * 8 + xq
        )

    def tok_start(dz):
        def step(j, c):
            tok_copy(dz, j).start()
            return c

        lax.fori_loop(1 if dz == 0 else 0, 8, step, 0)

    for dz in (2, 1, 3, 0):
        tok_start(dz)
    rbuf[dp] = sbuf[xc, zl]

    def kron(g, c):
        half = g // 2
        dz = jnp.where(half < 2, half, 5 - half)
        for s in range(GROUP):
            j = lax.rem(g, 2) * GROUP + s
            src = lax.rem(zl + 4 - dz, 4) * 8 + lax.rem(xc + 8 - j, 8)

            def arrived():
                remote(
                    sbuf.at[0, 0], rbuf.at[src], t_ss.at[0], t_rs.at[src], dp=src
                ).wait_recv()

            if s == 0:
                pl.when(g > 0)(arrived)
            else:
                arrived()
            xr = rbuf[src, 0:HALF, :].astype(F32)
            gr = rbuf[src, HALF:R, :].astype(F32)
            lanes = slice(128 * s, 128 * (s + 1))
            for i in range(HALF):
                outer[HALF * i : HALF * (i + 1), lanes] = (xr[i : i + 1, :] * gr).astype(BF)
            ids = rbuf[src, R : R + 8, :].astype(F32)[0:1, :].astype(jnp.int32)
            member[:, lanes] = (
                (ids == lax.broadcasted_iota(jnp.int32, (EX, 128), 0) + 1).astype(F32).astype(BF)
            )
        acc[...] += nt(outer[...], member[...])
        return c

    lax.fori_loop(0, 32 // GROUP, kron, 0)

    yp, ym = at_y(1), at_y(3)
    before, after, across = lax.rem(y + 3, 4), lax.rem(y + 1, 4), lax.rem(y + 2, 4)
    r = lax.rem(x + 4 - 2 * zh, 4)
    mine = jnp.where(r < 2, r, 3 - r)
    other = 1 - mine
    twin = dp + 1 - 2 * core

    def at_x(k):
        return zl * 8 + lax.rem(x + k, 4) * 2 + core

    def b_copy(q, n, way):
        return remote(
            bbuf.at[q, n], bbuf.at[q, n], b_ss.at[q, n, way], b_rs.at[q, n], tensor=yp if way == 0 else ym
        )

    def b_wait(q, n):
        b_copy(q, n, 0).wait_recv()

    def a_first(n, side):
        return remote(
            bbuf.at[y, n], abuf.at[mine * 2 + core, n], a_ss.at[side, n], a_rs.at[mine, n],
            dp=at_x(1 if side == 0 else 3),
        )

    def a_next(n):
        slot = abuf.at[mine * 2 + core, n]
        return remote(slot, slot, a_ss.at[0, n], a_rs.at[mine, n], dp=at_x(1 + 2 * (r - 2)))

    def a_wait(which, n):
        slot = abuf.at[which * 2 + core, n]
        remote(slot, slot, a_ss.at[0, n], a_rs.at[which, n], dp=at_x(1)).wait_recv()

    def x_copy(which, n):
        slot = abuf.at[which * 2 + core, n]
        return remote(slot, slot, x_ss.at[which, n], x_rs.at[which, n], dp=twin)

    def x_wait(which):
        for n in range(CHUNKS):
            slot = abuf.at[which * 2 + 1 - core, n]
            remote(slot, slot, x_ss.at[which, n], x_rs.at[which, n], dp=twin).wait_recv()

    scale = 1.0 / jnp.maximum(acc[COLS : COLS + 1, :], 1.0)
    for n in range(CHUNKS):
        piece = (acc[WIDE * n : WIDE * (n + 1), :] * scale).T.astype(BF)
        bbuf[y, n] = piece

        @pl.when(r < 2)
        def _():
            a_first(n, 0).start()
            a_first(n, 1).start()
            abuf[mine * 2 + core, n] = piece
            x_copy(mine, n).start()

        b_copy(y, n, 0).start()
        b_copy(y, n, 1).start()

    def c_copy(q, which):
        rows = pl.ds(pl.multiple_of(2 * EX * which, 2 * EX), 2 * EX)
        return remote(
            c_send.at[q, rows], c_recv.at[zl, rows], c_ss.at[q, which], c_rs.at[zl, which],
            dp=q * 8 + x * 2 + core,
        )

    def block(which, q):
        rows = pl.ds(pl.multiple_of(2 * EX * which, 2 * EX), 2 * EX)
        product = jnp.zeros((2 * EX, EX), F32)
        for n in range(CHUNKS):
            product = product + nt(abuf[pl.ds(which * 2, 2), n].reshape(2 * EX, WIDE), bbuf[q, n])
        product = product * (1.0 / R)

        @pl.when(q == zl)
        def _():
            keep[rows, :] = product

        @pl.when(q != zl)
        def _():
            c_send[q, rows, :] = product.astype(BF)
            c_copy(q, which).start()

    @pl.when(r < 2)
    def _():
        x_wait(mine)
        block(mine, y)

    for n in range(CHUNKS):
        @pl.when(r >= 2)
        def _():
            a_wait(mine, n)
            a_next(n).start()
            x_copy(mine, n).start()

        b_wait(before, n)
        if n < CHUNKS // 2:
            b_copy(before, n, 0).start()
        b_wait(after, n)
        if n >= CHUNKS // 2:
            b_copy(after, n, 1).start()

    @pl.when(r >= 2)
    def _():
        x_wait(mine)
        block(mine, y)

    block(mine, after)
    block(mine, before)
    for n in range(CHUNKS):
        a_wait(other, n)
        x_copy(other, n).start()
    x_wait(other)
    block(other, y)
    block(other, after)
    block(other, before)
    for n in range(CHUNKS):
        b_wait(across, n)
    block(mine, across)
    block(other, across)

    result = keep[...]
    for k in range(1, 4):
        src = lax.rem(zl + k, 4)
        for which in range(2):
            rows = slice(2 * EX * which, 2 * EX * (which + 1))
            remote(
                c_send.at[src, rows], c_recv.at[src, rows], c_ss.at[src, which], c_rs.at[src, which],
                dp=src * 8 + x * 2 + core,
            ).wait_recv()
        result = result + c_recv[src].astype(F32)
    out[...] = result

    def left(k, c):
        tok_copy(k // 8, lax.rem(k, 8)).wait_send()
        return c

    lax.fori_loop(1, 32, left, 0)
    for k in range(3):
        rs_copy(k).wait_send()
        for h in range(2):
            v_copy(h, k + 1).wait_send()
            c_copy(lax.rem(zl + k + 1, 4), h).wait_send()
    for h in range(2):
        z_copy(h).wait_send()
    for n in range(CHUNKS):
        b_copy(y, n, 0).wait_send()
        b_copy(y, n, 1).wait_send()
        if n < CHUNKS // 2:
            b_copy(before, n, 0).wait_send()
        else:
            b_copy(after, n, 1).wait_send()
        x_copy(0, n).wait_send()
        x_copy(1, n).wait_send()

        @pl.when(r < 2)
        def _():
            a_first(n, 0).wait_send()
            a_first(n, 1).wait_send()

        @pl.when(r >= 2)
        def _():
            a_next(n).wait_send()


def body(hidden, out_grad, proj_in, proj_out, owner_ids, example_ids):
    wide, model = hidden.shape[1], out_grad.shape[1]
    hbm = pl.BlockSpec(memory_space=pltpu.HBM)
    vmem = pl.BlockSpec(memory_space=pltpu.VMEM)
    dma = pltpu.SemaphoreType.DMA
    return pl.pallas_call(
        kernel,
        out_shape=jax.ShapeDtypeStruct((4 * EX, EX), F32),
        in_specs=[hbm] * 6,
        out_specs=vmem,
        scratch_shapes=[
            pltpu.VMEM((1, TOK), jnp.int32),
            pltpu.VMEM((1, TOK), jnp.int32),
            pltpu.VMEM((4, PART, wide), BF),
            pltpu.VMEM((4, PART, model), BF),
            pltpu.VMEM((R, wide), BF),
            pltpu.VMEM((R, model), BF),
            pltpu.VMEM((2, 2 * R, 128), F32),
            pltpu.VMEM((3, 2, 2 * R, 128), BF),
            pltpu.VMEM((4, 2, 2 * R, 128), BF),
            pltpu.VMEM((2, 2 * R, 128), BF),
            pltpu.VMEM((2, 2 * R, 128), BF),
            pltpu.VMEM((2, 4, 2 * R, 128), BF),
            pltpu.VMEM((8 * 128, TOK), BF),
            pltpu.VMEM((2 * R, 8 * 128), F32),
            pltpu.VMEM((8, 4, R + 8, 128), BF),
            pltpu.VMEM((32, R + 8, 128), BF),
            pltpu.VMEM((COLS + 16, 128 * GROUP), BF),
            pltpu.VMEM((EX, 128 * GROUP), BF),
            pltpu.VMEM((COLS + 16, EX), F32),
            pltpu.VMEM((4, CHUNKS, EX, WIDE), BF),
            pltpu.VMEM((4, CHUNKS, EX, WIDE), BF),
            pltpu.VMEM((4 * EX, EX), F32),
            pltpu.VMEM((4, 4 * EX, EX), BF),
            pltpu.VMEM((4, 4 * EX, EX), BF),
            dma((4,)), dma((4,)), dma((4,)), dma((3,)), dma((4,)), dma((2,)), dma((2,)),
            dma((2, 4)), dma((2, 4)), dma((32,)), dma((32,)),
            dma((2, CHUNKS)), dma((2, CHUNKS)), dma((2, CHUNKS)), dma((2, CHUNKS)),
            dma((4, CHUNKS, 2)), dma((4, CHUNKS)), dma((4, 2)), dma((4, 2)),
        ],
        compiler_params=pltpu.CompilerParams(
            collective_id=0, has_side_effects=True, vmem_limit_bytes=60 * 1024 * 1024
        ),
        name="per_example_kernel",
    )(hidden, out_grad, proj_in.T, proj_out.T, owner_ids.reshape(1, TOK), example_ids.reshape(1, TOK))


def solution(mesh):
    in_specs = (
        P("dp", "tensor"),
        P("dp", "tensor"),
        P("tensor", None),
        P("tensor", None),
        P("dp", None),
        P("dp"),
    )
    out_specs = P("tensor", "dp")
    return jax.shard_map(body, mesh=mesh, in_specs=in_specs, out_specs=out_specs, check_vma=False)
```

```python
import jax
import jax.numpy as jnp
from jax import lax
from jax.experimental import pallas as pl
from jax.experimental.pallas import tpu as pltpu
from jax.sharding import PartitionSpec as P

TOK = 1024
PART = 256
EX = 128
R = 64
HALF = 32
COLS = HALF * HALF
GROUP = 4
CHUNKS = 4
WIDE = COLS // CHUNKS
NT = (((1,), (1,)), ((), ()))
MESH = pl.DeviceIdType.MESH
BF = jnp.bfloat16
F32 = jnp.float32


def nt(a, b):
    return lax.dot_general(a, b, NT, preferred_element_type=F32)


def kernel(
    hid, og, pin, pout, own_in, exi_in, out,
    own, exi,
    hbuf, gbuf, pinb, poutb, part_own, rs_send, rs_recv, z_send, z_recv, vals, slots,
    routed, ids_send, ids_recv, sbuf, rbuf, outer, member, acc, bbuf, abuf, keep, sums, c_send, c_recv,
    hsem, gsem, psem, rs_ss, rs_rs, z_ss, z_rs, v_ss, v_rs, i_ss, i_rs, t_ss, t_rs,
    a_ss, a_rs, x_ss, x_rs, b_ss, b_rs, c_ss, c_rs,
):
    dp = lax.axis_index("dp")
    tn = lax.axis_index("tensor")
    y = tn // 2
    zh = lax.rem(tn, 2)
    zl = dp // 8
    x = lax.rem(dp // 2, 4)
    core = lax.rem(dp, 2)

    def remote(src, dst, ss, rs, **where):
        return pltpu.make_async_remote_copy(
            src_ref=src, dst_ref=dst, send_sem=ss, recv_sem=rs,
            device_id=where, device_id_type=MESH,
        )

    def at_y(k):
        return lax.rem(y + k, 4) * 2 + zh

    cp_in = pltpu.make_async_copy(pin, pinb, psem.at[0])
    cp_out = pltpu.make_async_copy(pout, poutb, psem.at[1])
    cp_own = pltpu.make_async_copy(own_in, own, psem.at[2])
    cp_exi = pltpu.make_async_copy(exi_in, exi, psem.at[3])
    cp_own.start()
    cp_exi.start()
    cp_out.start()
    cp_in.start()

    def load(k):
        p = lax.rem(y + 1 + k, 4)
        rows = pl.ds(pl.multiple_of(p * PART, PART), PART)
        return (
            pltpu.make_async_copy(og.at[rows], gbuf.at[p], gsem.at[k]),
            pltpu.make_async_copy(hid.at[rows], hbuf.at[p], hsem.at[k]),
        )

    for k in range(4):
        for cp in load(k):
            cp.start()

    barrier = pltpu.get_barrier_semaphore()

    def greet(k, c):
        pl.semaphore_signal(barrier, inc=1, device_id={"dp": lax.rem(dp + k, 32)}, device_id_type=MESH)
        return c

    lax.fori_loop(1, 32, greet, 0)
    for k in range(1, 4):
        pl.semaphore_signal(barrier, inc=1, device_id={"tensor": at_y(k)}, device_id_type=MESH)
    pl.semaphore_signal(barrier, inc=1, device_id={"tensor": y * 2 + 1 - zh}, device_id_type=MESH)

    cp_own.wait()
    cp_exi.wait()
    hot = (own[...] - 8 * y == lax.broadcasted_iota(jnp.int32, (8, TOK), 0)).astype(F32)
    tri = (
        lax.broadcasted_iota(jnp.int32, (128, 128), 0) <= lax.broadcasted_iota(jnp.int32, (128, 128), 1)
    ).astype(BF)
    first = (lax.broadcasted_iota(jnp.int32, (8, 128), 0) * 128).astype(F32)
    carry = jnp.zeros((8, 1), F32)
    keys = []
    for b in range(8):
        h = hot[:, 128 * b : 128 * (b + 1)]
        rank = jnp.dot(h.astype(BF), tri, preferred_element_type=F32) + carry
        carry = carry + jnp.sum(h, 1, keepdims=True)
        keys.append(jnp.sum(h * (first + rank), 0, keepdims=True))
    order = [2 * p + ch for ch in range(2) for p in range(4)]
    key = jnp.concatenate([keys[b] for b in order], 1).astype(jnp.int32) - 1
    idrow = (exi[...] + 1).astype(F32)
    idrow = jnp.concatenate([idrow[:, 128 * b : 128 * (b + 1)] for b in order], 1)
    idrow = jnp.broadcast_to(idrow, (16, TOK)).astype(BF)
    for o in range(8):
        hit = key == lax.broadcasted_iota(jnp.int32, (128, TOK), 0) + 128 * o
        slots[128 * o : 128 * (o + 1), :] = hit.astype(F32).astype(BF)
        ids = nt(idrow, slots[128 * o : 128 * (o + 1), :])[0:8, :].astype(BF)
        ids_send[o] = ids
    outer[COLS : COLS + 16, :] = jnp.ones((16, 128 * GROUP), BF)
    acc[...] = jnp.zeros_like(acc)

    def rs_copy(k, ch):
        p = lax.rem(y + 1 + k, 4)
        return remote(
            rs_send.at[k, ch], rs_recv.at[y, ch], rs_ss.at[k, ch], rs_rs.at[y, ch], tensor=p * 2 + zh
        )

    def project(k):
        p = lax.rem(y + 1 + k, 4)
        for cp in load(k):
            cp.wait()
        gp = nt(gbuf[p], poutb[...])
        xp = nt(hbuf[p], pinb[...])
        return jnp.concatenate([xp, gp], 1).T

    cp_out.wait()
    cp_in.wait()
    xc = lax.rem(dp, 8)

    def ids_copy(dz, j):
        zq, xq = lax.rem(zl + dz, 4), lax.rem(xc + j, 8)
        return remote(
            ids_send.at[xq], ids_recv.at[dp], i_ss.at[dz * 8 + j], i_rs.at[dp], dp=zq * 8 + xq
        )

    def ids_start(k, c):
        ids_copy(k // 8, lax.rem(k, 8)).start()
        return c

    for k in range(3):
        both = project(k).astype(BF)
        rs_send[k, 0] = both[:, :128]
        rs_send[k, 1] = both[:, 128:]
        if k == 0:
            pl.semaphore_wait(barrier, 35)
        rs_copy(k, 0).start()
        rs_copy(k, 1).start()
    both = project(3)
    part_own[0] = both[:, :128]
    part_own[1] = both[:, 128:]

    def z_copy(ch):
        return remote(z_send.at[ch], z_recv.at[ch], z_ss.at[ch], z_rs.at[ch], tensor=y * 2 + 1 - zh)

    for ch in range(2):
        total = part_own[ch]
        for k in range(1, 4):
            src = lax.rem(y + k, 4)
            remote(
                rs_send.at[0, ch], rs_recv.at[src, ch], rs_ss.at[0, ch], rs_rs.at[src, ch],
                tensor=src * 2 + zh,
            ).wait_recv()
            total = total + rs_recv[src, ch].astype(F32)
        z_send[ch] = total.astype(BF)
        z_copy(ch).start()
        part_own[ch] = total

    lax.fori_loop(1, 32, ids_start, 0)
    ids_recv[dp] = ids_send[xc]

    def v_copy(ch, k):
        return remote(vals.at[ch, y], vals.at[ch, y], v_ss.at[ch, k], v_rs.at[ch, y], tensor=at_y(k))

    for ch in range(2):
        z_copy(ch).wait_recv()
        vals[ch, y] = (part_own[ch] + z_recv[ch].astype(F32)).astype(BF)
        for k in range(1, 4):
            v_copy(ch, k).start()

    for ch in range(2):
        for k in range(1, 4):
            src = lax.rem(y + k, 4)
            remote(
                vals.at[ch, src], vals.at[ch, src], v_ss.at[ch, k], v_rs.at[ch, src], tensor=at_y(k)
            ).wait_recv()
        part = jnp.concatenate([vals[ch, p] for p in range(4)], 1)
        for b in range(2):
            rows = slice(512 * b, 512 * (b + 1))
            placed = nt(part, slots[rows, 512 * ch : 512 * (ch + 1)])
            if ch == 0:
                routed[:, rows] = placed
                continue
            placed = (placed + routed[:, rows]).astype(BF)
            for o in range(4):
                piece = placed[:, 128 * o : 128 * (o + 1)]
                for q in range(4):
                    sbuf[4 * b + o, q, 0:HALF, :] = piece[HALF * (q // 2) : HALF * (q // 2 + 1), :]
                    sbuf[4 * b + o, q, HALF:R, :] = piece[R + HALF * (q % 2) : R + HALF * (q % 2 + 1), :]


    def tok_copy(dz, j):
        zq, xq = lax.rem(zl + dz, 4), lax.rem(xc + j, 8)
        return remote(
            sbuf.at[xq, zq], rbuf.at[dp], t_ss.at[dz * 8 + j], t_rs.at[dp], dp=zq * 8 + xq
        )

    def tok_start(dz):
        def step(j, c):
            tok_copy(dz, j).start()
            return c

        lax.fori_loop(1 if dz == 0 else 0, 8, step, 0)

    for dz in (1, 3, 2, 0):
        tok_start(dz)
    rbuf[dp] = sbuf[xc, zl]

    def kron(g, c):
        half = g // 2
        dz = jnp.where(half < 2, half, 5 - half)
        for s in range(GROUP):
            j = lax.rem(g, 2) * GROUP + s
            src = lax.rem(zl + 4 - dz, 4) * 8 + lax.rem(xc + 8 - j, 8)

            def arrived():
                remote(
                    ids_send.at[0], ids_recv.at[src], i_ss.at[0], i_rs.at[src], dp=src
                ).wait_recv()
                remote(
                    sbuf.at[0, 0], rbuf.at[src], t_ss.at[0], t_rs.at[src], dp=src
                ).wait_recv()

            if s == 0:
                pl.when(g > 0)(arrived)
            else:
                arrived()
            xr = rbuf[src, 0:HALF, :].astype(F32)
            gr = rbuf[src, HALF:R, :].astype(F32)
            lanes = slice(128 * s, 128 * (s + 1))
            for i in range(HALF):
                outer[HALF * i : HALF * (i + 1), lanes] = (xr[i : i + 1, :] * gr).astype(BF)
            ids = ids_recv[src].astype(F32)[0:1, :].astype(jnp.int32)
            member[:, lanes] = (
                (ids == lax.broadcasted_iota(jnp.int32, (EX, 128), 0) + 1).astype(F32).astype(BF)
            )
        acc[...] += nt(outer[...], member[...])
        return c

    lax.fori_loop(0, 32 // GROUP, kron, 0)

    yp, ym = at_y(1), at_y(3)
    before, after, across = lax.rem(y + 3, 4), lax.rem(y + 1, 4), lax.rem(y + 2, 4)
    r = lax.rem(x + 4 - 2 * zh, 4)
    mine = jnp.where(r < 2, r, 3 - r)
    other = 1 - mine
    twin = dp + 1 - 2 * core

    def at_x(k):
        return zl * 8 + lax.rem(x + k, 4) * 2 + core

    def b_copy(q, n, way):
        return remote(
            bbuf.at[q, n], bbuf.at[q, n], b_ss.at[q, n, way], b_rs.at[q, n], tensor=yp if way == 0 else ym
        )

    def b_wait(q, n):
        b_copy(q, n, 0).wait_recv()

    def a_first(n, side):
        return remote(
            bbuf.at[y, n], abuf.at[mine * 2 + core, n], a_ss.at[side, n], a_rs.at[mine, n],
            dp=at_x(1 if side == 0 else 3),
        )

    def a_next(n):
        slot = abuf.at[mine * 2 + core, n]
        return remote(slot, slot, a_ss.at[0, n], a_rs.at[mine, n], dp=at_x(1 + 2 * (r - 2)))

    def a_wait(which, n):
        slot = abuf.at[which * 2 + core, n]
        remote(slot, slot, a_ss.at[0, n], a_rs.at[which, n], dp=at_x(1)).wait_recv()

    def x_copy(which, n):
        slot = abuf.at[which * 2 + core, n]
        return remote(slot, slot, x_ss.at[which, n], x_rs.at[which, n], dp=twin)

    def x_wait(which, n):
        slot = abuf.at[which * 2 + 1 - core, n]
        remote(slot, slot, x_ss.at[which, n], x_rs.at[which, n], dp=twin).wait_recv()

    scale = 1.0 / jnp.maximum(acc[COLS : COLS + 1, :], 1.0)
    for n in range(CHUNKS):
        piece = (acc[WIDE * n : WIDE * (n + 1), :] * scale).T.astype(BF)
        bbuf[y, n] = piece

        @pl.when(r < 2)
        def _():
            a_first(n, 0).start()
            a_first(n, 1).start()
            abuf[mine * 2 + core, n] = piece
            x_copy(mine, n).start()

        b_copy(y, n, 0).start()
        b_copy(y, n, 1).start()

    def c_copy(q, which):
        rows = pl.ds(pl.multiple_of(2 * EX * which, 2 * EX), 2 * EX)
        return remote(
            c_send.at[q, rows], c_recv.at[zl, rows], c_ss.at[q, which], c_rs.at[zl, which],
            dp=q * 8 + x * 2 + core,
        )

    def term(which, q, n):
        return nt(abuf[pl.ds(which * 2, 2), n].reshape(2 * EX, WIDE), bbuf[q, n])

    def block(which, q, product=None, begin=0):
        rows = pl.ds(pl.multiple_of(2 * EX * which, 2 * EX), 2 * EX)
        for n in range(begin, CHUNKS):
            product = term(which, q, n) if product is None else product + term(which, q, n)
        product = product * (1.0 / R)

        @pl.when(q == zl)
        def _():
            keep[rows, :] = product

        @pl.when(q != zl)
        def _():
            c_send[q, rows, :] = product.astype(BF)
            c_copy(q, which).start()

    @pl.when(r < 2)
    def _():
        for n in range(CHUNKS):
            x_wait(mine, n)
        block(mine, y)

    for n in range(CHUNKS):
        @pl.when(r >= 2)
        def _():
            a_wait(mine, n)
            a_next(n).start()
            x_copy(mine, n).start()

        b_wait(before, n)
        if n < CHUNKS // 2:
            b_copy(before, n, 0).start()
        b_wait(after, n)
        if n >= CHUNKS // 2:
            b_copy(after, n, 1).start()

    @pl.when(r >= 2)
    def _():
        for n in range(CHUNKS):
            x_wait(mine, n)
        block(mine, y)

    block(mine, after)
    block(mine, before)
    near = (y, after, before)
    for n in range(CHUNKS):
        a_wait(other, n)
        x_copy(other, n).start()
        if n > 0:
            x_wait(other, n - 1)
            for t in range(3):
                new = term(other, near[t], n - 1)
                sums[t] = new if n == 1 else sums[t] + new
    for n in range(CHUNKS):
        b_wait(across, n)
    block(mine, across)
    x_wait(other, CHUNKS - 1)
    for t in range(3):
        block(other, near[t], sums[t], CHUNKS - 1)
    block(other, across)

    for which in range(2):
        rows = slice(2 * EX * which, 2 * EX * (which + 1))
        result = keep[rows, :]
        for k in range(1, 4):
            src = lax.rem(zl + k, 4)
            remote(
                c_send.at[src, rows], c_recv.at[src, rows], c_ss.at[src, which], c_rs.at[src, which],
                dp=src * 8 + x * 2 + core,
            ).wait_recv()
            result = result + c_recv[src, rows, :].astype(F32)
        out[rows, :] = result

    def left(k, c):
        tok_copy(k // 8, lax.rem(k, 8)).wait_send()
        ids_copy(k // 8, lax.rem(k, 8)).wait_send()
        return c

    lax.fori_loop(1, 32, left, 0)
    for k in range(3):
        rs_copy(k, 0).wait_send()
        rs_copy(k, 1).wait_send()
        for h in range(2):
            v_copy(h, k + 1).wait_send()
            c_copy(lax.rem(zl + k + 1, 4), h).wait_send()
    for h in range(2):
        z_copy(h).wait_send()
    for n in range(CHUNKS):
        b_copy(y, n, 0).wait_send()
        b_copy(y, n, 1).wait_send()
        if n < CHUNKS // 2:
            b_copy(before, n, 0).wait_send()
        else:
            b_copy(after, n, 1).wait_send()
        x_copy(0, n).wait_send()
        x_copy(1, n).wait_send()

        @pl.when(r < 2)
        def _():
            a_first(n, 0).wait_send()
            a_first(n, 1).wait_send()

        @pl.when(r >= 2)
        def _():
            a_next(n).wait_send()


def body(hidden, out_grad, proj_in, proj_out, owner_ids, example_ids):
    wide, model = hidden.shape[1], out_grad.shape[1]
    hbm = pl.BlockSpec(memory_space=pltpu.HBM)
    vmem = pl.BlockSpec(memory_space=pltpu.VMEM)
    dma = pltpu.SemaphoreType.DMA
    return pl.pallas_call(
        kernel,
        out_shape=jax.ShapeDtypeStruct((4 * EX, EX), F32),
        in_specs=[hbm] * 6,
        out_specs=vmem,
        scratch_shapes=[
            pltpu.VMEM((1, TOK), jnp.int32),
            pltpu.VMEM((1, TOK), jnp.int32),
            pltpu.VMEM((4, PART, wide), BF),
            pltpu.VMEM((4, PART, model), BF),
            pltpu.VMEM((R, wide), BF),
            pltpu.VMEM((R, model), BF),
            pltpu.VMEM((2, 2 * R, 128), F32),
            pltpu.VMEM((3, 2, 2 * R, 128), BF),
            pltpu.VMEM((4, 2, 2 * R, 128), BF),
            pltpu.VMEM((2, 2 * R, 128), BF),
            pltpu.VMEM((2, 2 * R, 128), BF),
            pltpu.VMEM((2, 4, 2 * R, 128), BF),
            pltpu.VMEM((8 * 128, TOK), BF),
            pltpu.VMEM((2 * R, 8 * 128), F32),
            pltpu.VMEM((8, 8, 128), BF),
            pltpu.VMEM((32, 8, 128), BF),
            pltpu.VMEM((8, 4, R, 128), BF),
            pltpu.VMEM((32, R, 128), BF),
            pltpu.VMEM((COLS + 16, 128 * GROUP), BF),
            pltpu.VMEM((EX, 128 * GROUP), BF),
            pltpu.VMEM((COLS + 16, EX), F32),
            pltpu.VMEM((4, CHUNKS, EX, WIDE), BF),
            pltpu.VMEM((4, CHUNKS, EX, WIDE), BF),
            pltpu.VMEM((4 * EX, EX), F32),
            pltpu.VMEM((3, 2 * EX, EX), F32),
            pltpu.VMEM((4, 4 * EX, EX), BF),
            pltpu.VMEM((4, 4 * EX, EX), BF),
            dma((4,)), dma((4,)), dma((4,)), dma((3, 2)), dma((4, 2)), dma((2,)), dma((2,)),
            dma((2, 4)), dma((2, 4)), dma((32,)), dma((32,)), dma((32,)), dma((32,)),
            dma((2, CHUNKS)), dma((2, CHUNKS)), dma((2, CHUNKS)), dma((2, CHUNKS)),
            dma((4, CHUNKS, 2)), dma((4, CHUNKS)), dma((4, 2)), dma((4, 2)),
        ],
        compiler_params=pltpu.CompilerParams(
            collective_id=0, has_side_effects=True, vmem_limit_bytes=60 * 1024 * 1024
        ),
        name="per_example_kernel",
    )(hidden, out_grad, proj_in.T, proj_out.T, owner_ids.reshape(1, TOK), example_ids.reshape(1, TOK))


def solution(mesh):
    in_specs = (
        P("dp", "tensor"),
        P("dp", "tensor"),
        P("tensor", None),
        P("tensor", None),
        P("dp", None),
        P("dp"),
    )
    out_specs = P("tensor", "dp")
    return jax.shard_map(body, mesh=mesh, in_specs=in_specs, out_specs=out_specs, check_vma=False)
```

```python
import jax
import jax.numpy as jnp
from jax import lax
from jax.experimental import pallas as pl
from jax.experimental.pallas import tpu as pltpu
from jax.sharding import PartitionSpec as P

TOK = 1024
PART = 256
EX = 128
R = 64
HALF = 32
COLS = HALF * HALF
GROUP = 4
CHUNKS = 4
WIDE = COLS // CHUNKS
NT = (((1,), (1,)), ((), ()))
MESH = pl.DeviceIdType.MESH
BF = jnp.bfloat16
F32 = jnp.float32


def nt(a, b):
    return lax.dot_general(a, b, NT, preferred_element_type=F32)


def kernel(
    hid, og, pin, pout, own_in, exi_in, out,
    own, exi,
    hbuf, gbuf, pinb, poutb, part_own, rs_send, rs_recv, z_send, z_recv, vals, slots,
    routed, ids_send, ids_recv, sbuf, rbuf, outer, member, acc, bbuf, abuf, keep, sums, c_send, c_recv,
    hsem, gsem, psem, rs_ss, rs_rs, z_ss, z_rs, v_ss, v_rs, i_ss, i_rs, t_ss, t_rs,
    a_ss, a_rs, x_ss, x_rs, b_ss, b_rs, c_ss, c_rs,
):
    dp = lax.axis_index("dp")
    tn = lax.axis_index("tensor")
    y = tn // 2
    zh = lax.rem(tn, 2)
    zl = dp // 8
    x = lax.rem(dp // 2, 4)
    core = lax.rem(dp, 2)

    def remote(src, dst, ss, rs, **where):
        return pltpu.make_async_remote_copy(
            src_ref=src, dst_ref=dst, send_sem=ss, recv_sem=rs,
            device_id=where, device_id_type=MESH,
        )

    def at_y(k):
        return lax.rem(y + k, 4) * 2 + zh

    cp_in = pltpu.make_async_copy(pin, pinb, psem.at[0])
    cp_out = pltpu.make_async_copy(pout, poutb, psem.at[1])
    cp_own = pltpu.make_async_copy(own_in, own, psem.at[2])
    cp_exi = pltpu.make_async_copy(exi_in, exi, psem.at[3])
    cp_own.start()
    cp_exi.start()
    cp_out.start()
    cp_in.start()

    def load(k):
        p = lax.rem(y + 1 + k, 4)
        rows = pl.ds(pl.multiple_of(p * PART, PART), PART)
        return (
            pltpu.make_async_copy(og.at[rows], gbuf.at[p], gsem.at[k]),
            pltpu.make_async_copy(hid.at[rows], hbuf.at[p], hsem.at[k]),
        )

    for k in range(4):
        for cp in load(k):
            cp.start()

    barrier = pltpu.get_barrier_semaphore()

    def greet(k, c):
        pl.semaphore_signal(barrier, inc=1, device_id={"dp": lax.rem(dp + k, 32)}, device_id_type=MESH)
        return c

    lax.fori_loop(1, 32, greet, 0)
    for k in range(1, 4):
        pl.semaphore_signal(barrier, inc=1, device_id={"tensor": at_y(k)}, device_id_type=MESH)
    pl.semaphore_signal(barrier, inc=1, device_id={"tensor": y * 2 + 1 - zh}, device_id_type=MESH)

    cp_own.wait()
    cp_exi.wait()
    hot = (own[...] - 8 * y == lax.broadcasted_iota(jnp.int32, (8, TOK), 0)).astype(F32)
    tri = (
        lax.broadcasted_iota(jnp.int32, (128, 128), 0) <= lax.broadcasted_iota(jnp.int32, (128, 128), 1)
    ).astype(BF)
    first = (lax.broadcasted_iota(jnp.int32, (8, 128), 0) * 128).astype(F32)
    carry = jnp.zeros((8, 1), F32)
    keys = []
    for b in range(8):
        h = hot[:, 128 * b : 128 * (b + 1)]
        rank = jnp.dot(h.astype(BF), tri, preferred_element_type=F32) + carry
        carry = carry + jnp.sum(h, 1, keepdims=True)
        keys.append(jnp.sum(h * (first + rank), 0, keepdims=True))
    order = [2 * p + ch for ch in range(2) for p in range(4)]
    key = jnp.concatenate([keys[b] for b in order], 1).astype(jnp.int32) - 1
    idrow = (exi[...] + 1).astype(F32)
    idrow = jnp.concatenate([idrow[:, 128 * b : 128 * (b + 1)] for b in order], 1)
    idrow = jnp.broadcast_to(idrow, (16, TOK)).astype(BF)
    for o in range(8):
        hit = key == lax.broadcasted_iota(jnp.int32, (128, TOK), 0) + 128 * o
        slots[128 * o : 128 * (o + 1), :] = hit.astype(F32).astype(BF)
        ids = nt(idrow, slots[128 * o : 128 * (o + 1), :])[0:8, :].astype(BF)
        ids_send[o] = ids
    outer[COLS : COLS + 16, :] = jnp.ones((16, 128 * GROUP), BF)
    acc[...] = jnp.zeros_like(acc)

    def rs_copy(k, ch):
        p = lax.rem(y + 1 + k, 4)
        return remote(
            rs_send.at[k, ch], rs_recv.at[y, ch], rs_ss.at[k, ch], rs_rs.at[y, ch], tensor=p * 2 + zh
        )

    def project(k):
        p = lax.rem(y + 1 + k, 4)
        for cp in load(k):
            cp.wait()
        gp = nt(gbuf[p], poutb[...])
        xp = nt(hbuf[p], pinb[...])
        return jnp.concatenate([xp, gp], 1).T

    cp_out.wait()
    cp_in.wait()
    xc = lax.rem(dp, 8)

    def ids_copy(dz, j):
        zq, xq = lax.rem(zl + dz, 4), lax.rem(xc + j, 8)
        return remote(
            ids_send.at[xq], ids_recv.at[dp], i_ss.at[dz * 8 + j], i_rs.at[dp], dp=zq * 8 + xq
        )

    def ids_start(k, c):
        ids_copy(k // 8, lax.rem(k, 8)).start()
        return c

    for k in range(3):
        both = project(k).astype(BF)
        rs_send[k, 0] = both[:, :128]
        rs_send[k, 1] = both[:, 128:]
        if k == 0:
            pl.semaphore_wait(barrier, 35)
        rs_copy(k, 0).start()
        rs_copy(k, 1).start()
    both = project(3)
    part_own[0] = both[:, :128]
    part_own[1] = both[:, 128:]

    def z_copy(ch):
        return remote(z_send.at[ch], z_recv.at[ch], z_ss.at[ch], z_rs.at[ch], tensor=y * 2 + 1 - zh)

    for ch in range(2):
        total = part_own[ch]
        for k in range(1, 4):
            src = lax.rem(y + k, 4)
            remote(
                rs_send.at[0, ch], rs_recv.at[src, ch], rs_ss.at[0, ch], rs_rs.at[src, ch],
                tensor=src * 2 + zh,
            ).wait_recv()
            total = total + rs_recv[src, ch].astype(F32)
        z_send[ch] = total.astype(BF)
        z_copy(ch).start()
        part_own[ch] = total

    lax.fori_loop(1, 32, ids_start, 0)
    ids_recv[dp] = ids_send[xc]

    def v_copy(ch, k):
        return remote(vals.at[ch, y], vals.at[ch, y], v_ss.at[ch, k], v_rs.at[ch, y], tensor=at_y(k))

    for ch in range(2):
        z_copy(ch).wait_recv()
        vals[ch, y] = (part_own[ch] + z_recv[ch].astype(F32)).astype(BF)
        for k in range(1, 4):
            v_copy(ch, k).start()

    for ch in range(2):
        for k in range(1, 4):
            src = lax.rem(y + k, 4)
            remote(
                vals.at[ch, src], vals.at[ch, src], v_ss.at[ch, k], v_rs.at[ch, src], tensor=at_y(k)
            ).wait_recv()
        part = jnp.concatenate([vals[ch, p] for p in range(4)], 1)
        for b in range(2):
            rows = slice(512 * b, 512 * (b + 1))
            placed = nt(part, slots[rows, 512 * ch : 512 * (ch + 1)])
            if ch == 0:
                routed[:, rows] = placed
                continue
            placed = (placed + routed[:, rows]).astype(BF)
            for o in range(4):
                piece = placed[:, 128 * o : 128 * (o + 1)]
                for q in range(4):
                    sbuf[4 * b + o, q, 0:HALF, :] = piece[HALF * (q // 2) : HALF * (q // 2 + 1), :]
                    sbuf[4 * b + o, q, HALF:R, :] = piece[R + HALF * (q % 2) : R + HALF * (q % 2 + 1), :]


    def tok_copy(dz, j):
        zq, xq = lax.rem(zl + dz, 4), lax.rem(xc + j, 8)
        return remote(
            sbuf.at[xq, zq], rbuf.at[dp], t_ss.at[dz * 8 + j], t_rs.at[dp], dp=zq * 8 + xq
        )

    def tok_start(dz):
        def step(j, c):
            tok_copy(dz, j).start()
            return c

        lax.fori_loop(1 if dz == 0 else 0, 8, step, 0)

    for dz in (1, 3, 2, 0):
        tok_start(dz)
    rbuf[dp] = sbuf[xc, zl]

    def kron(g, c):
        half = g // 2
        dz = jnp.where(half < 2, half, 5 - half)
        for s in range(GROUP):
            j = lax.rem(g, 2) * GROUP + s
            src = lax.rem(zl + 4 - dz, 4) * 8 + lax.rem(xc + 8 - j, 8)

            def arrived():
                remote(
                    ids_send.at[0], ids_recv.at[src], i_ss.at[0], i_rs.at[src], dp=src
                ).wait_recv()
                remote(
                    sbuf.at[0, 0], rbuf.at[src], t_ss.at[0], t_rs.at[src], dp=src
                ).wait_recv()

            if s == 0:
                pl.when(g > 0)(arrived)
            else:
                arrived()
            xr = rbuf[src, 0:HALF, :].astype(F32)
            gr = rbuf[src, HALF:R, :].astype(F32)
            lanes = slice(128 * s, 128 * (s + 1))
            for i in range(HALF):
                outer[HALF * i : HALF * (i + 1), lanes] = (xr[i : i + 1, :] * gr).astype(BF)
            ids = ids_recv[src].astype(F32)[0:1, :].astype(jnp.int32)
            member[:, lanes] = (
                (ids == lax.broadcasted_iota(jnp.int32, (EX, 128), 0) + 1).astype(F32).astype(BF)
            )
        acc[...] += nt(outer[...], member[...])
        return c

    lax.fori_loop(0, 32 // GROUP, kron, 0)

    yp, ym = at_y(1), at_y(3)
    before, after, across = lax.rem(y + 3, 4), lax.rem(y + 1, 4), lax.rem(y + 2, 4)
    r = lax.rem(x + 4 - 2 * zh, 4)
    mine = jnp.where(r < 2, r, 3 - r)
    other = 1 - mine
    twin = dp + 1 - 2 * core

    def at_x(k):
        return zl * 8 + lax.rem(x + k, 4) * 2 + core

    def b_copy(q, n, way):
        return remote(
            bbuf.at[q, n], bbuf.at[q, n], b_ss.at[q, n, way], b_rs.at[q, n], tensor=yp if way == 0 else ym
        )

    def b_wait(q, n):
        b_copy(q, n, 0).wait_recv()

    def a_first(n, side):
        return remote(
            bbuf.at[y, n], abuf.at[mine * 2 + core, n], a_ss.at[side, n], a_rs.at[mine, n],
            dp=at_x(1 if side == 0 else 3),
        )

    def a_next(n):
        slot = abuf.at[mine * 2 + core, n]
        return remote(slot, slot, a_ss.at[0, n], a_rs.at[mine, n], dp=at_x(1 + 2 * (r - 2)))

    def a_wait(which, n):
        slot = abuf.at[which * 2 + core, n]
        remote(slot, slot, a_ss.at[0, n], a_rs.at[which, n], dp=at_x(1)).wait_recv()

    def x_copy(which, n):
        slot = abuf.at[which * 2 + core, n]
        return remote(slot, slot, x_ss.at[which, n], x_rs.at[which, n], dp=twin)

    def x_wait(which, n):
        slot = abuf.at[which * 2 + 1 - core, n]
        remote(slot, slot, x_ss.at[which, n], x_rs.at[which, n], dp=twin).wait_recv()

    scale = 1.0 / jnp.maximum(acc[COLS : COLS + 1, :], 1.0)
    for n in range(CHUNKS):
        piece = (acc[WIDE * n : WIDE * (n + 1), :] * scale).T.astype(BF)
        bbuf[y, n] = piece

        @pl.when(r < 2)
        def _():
            a_first(n, 0).start()
            a_first(n, 1).start()
            abuf[mine * 2 + core, n] = piece
            x_copy(mine, n).start()

        b_copy(y, n, 0).start()
        b_copy(y, n, 1).start()

    def c_copy(q, which):
        rows = pl.ds(pl.multiple_of(2 * EX * which, 2 * EX), 2 * EX)
        return remote(
            c_send.at[q, rows], c_recv.at[zl, rows], c_ss.at[q, which], c_rs.at[zl, which],
            dp=q * 8 + x * 2 + core,
        )

    def term(which, q, n):
        return nt(abuf[pl.ds(which * 2, 2), n].reshape(2 * EX, WIDE), bbuf[q, n])

    def block(which, q, product=None, begin=0):
        rows = pl.ds(pl.multiple_of(2 * EX * which, 2 * EX), 2 * EX)
        for n in range(begin, CHUNKS):
            product = term(which, q, n) if product is None else product + term(which, q, n)
        product = product * (1.0 / R)

        @pl.when(q == zl)
        def _():
            keep[rows, :] = product

        @pl.when(q != zl)
        def _():
            c_send[q, rows, :] = product.astype(BF)
            c_copy(q, which).start()

    @pl.when(r < 2)
    def _():
        for n in range(CHUNKS):
            x_wait(mine, n)
        block(mine, y)

    for n in range(CHUNKS):
        @pl.when(r >= 2)
        def _():
            for m in ((0, 1, 2, 3), (), (), ())[n]:
                a_wait(mine, m)
                a_next(m).start()
                x_copy(mine, m).start()

        b_wait(before, n)
        if n < CHUNKS // 2:
            b_copy(before, n, 0).start()
        b_wait(after, n)
        if n >= CHUNKS // 2:
            b_copy(after, n, 1).start()

    @pl.when(r >= 2)
    def _():
        for n in range(CHUNKS):
            x_wait(mine, n)
        block(mine, y)

    block(mine, after)
    block(mine, before)
    near = (y, after, before)
    for n in range(CHUNKS):
        a_wait(other, n)
        x_copy(other, n).start()
        if n > 0:
            x_wait(other, n - 1)
            for t in range(3):
                new = term(other, near[t], n - 1)
                sums[near[t]] = new if n == 1 else sums[near[t]] + new
    for n in range(CHUNKS):
        b_wait(across, n)
    block(mine, across)
    partial = term(other, across, 0)
    for n in range(1, CHUNKS - 1):
        partial = partial + term(other, across, n)
    sums[across] = partial
    x_wait(other, CHUNKS - 1)
    for k in (2, 1, 3, 0):
        q = lax.rem(zl + k, 4)
        block(other, q, sums[q], CHUNKS - 1)

    for which in range(2):
        rows = slice(2 * EX * which, 2 * EX * (which + 1))
        result = keep[rows, :]
        for k in range(1, 4):
            src = lax.rem(zl + k, 4)
            remote(
                c_send.at[src, rows], c_recv.at[src, rows], c_ss.at[src, which], c_rs.at[src, which],
                dp=src * 8 + x * 2 + core,
            ).wait_recv()
            result = result + c_recv[src, rows, :].astype(F32)
        out[rows, :] = result

    def left(k, c):
        tok_copy(k // 8, lax.rem(k, 8)).wait_send()
        ids_copy(k // 8, lax.rem(k, 8)).wait_send()
        return c

    lax.fori_loop(1, 32, left, 0)
    for k in range(3):
        rs_copy(k, 0).wait_send()
        rs_copy(k, 1).wait_send()
        for h in range(2):
            v_copy(h, k + 1).wait_send()
            c_copy(lax.rem(zl + k + 1, 4), h).wait_send()
    for h in range(2):
        z_copy(h).wait_send()
    for n in range(CHUNKS):
        b_copy(y, n, 0).wait_send()
        b_copy(y, n, 1).wait_send()
        if n < CHUNKS // 2:
            b_copy(before, n, 0).wait_send()
        else:
            b_copy(after, n, 1).wait_send()
        x_copy(0, n).wait_send()
        x_copy(1, n).wait_send()

        @pl.when(r < 2)
        def _():
            a_first(n, 0).wait_send()
            a_first(n, 1).wait_send()

        @pl.when(r >= 2)
        def _():
            a_next(n).wait_send()


def body(hidden, out_grad, proj_in, proj_out, owner_ids, example_ids):
    wide, model = hidden.shape[1], out_grad.shape[1]
    hbm = pl.BlockSpec(memory_space=pltpu.HBM)
    vmem = pl.BlockSpec(memory_space=pltpu.VMEM)
    dma = pltpu.SemaphoreType.DMA
    return pl.pallas_call(
        kernel,
        out_shape=jax.ShapeDtypeStruct((4 * EX, EX), F32),
        in_specs=[hbm] * 6,
        out_specs=vmem,
        scratch_shapes=[
            pltpu.VMEM((1, TOK), jnp.int32),
            pltpu.VMEM((1, TOK), jnp.int32),
            pltpu.VMEM((4, PART, wide), BF),
            pltpu.VMEM((4, PART, model), BF),
            pltpu.VMEM((R, wide), BF),
            pltpu.VMEM((R, model), BF),
            pltpu.VMEM((2, 2 * R, 128), F32),
            pltpu.VMEM((3, 2, 2 * R, 128), BF),
            pltpu.VMEM((4, 2, 2 * R, 128), BF),
            pltpu.VMEM((2, 2 * R, 128), BF),
            pltpu.VMEM((2, 2 * R, 128), BF),
            pltpu.VMEM((2, 4, 2 * R, 128), BF),
            pltpu.VMEM((8 * 128, TOK), BF),
            pltpu.VMEM((2 * R, 8 * 128), F32),
            pltpu.VMEM((8, 8, 128), BF),
            pltpu.VMEM((32, 8, 128), BF),
            pltpu.VMEM((8, 4, R, 128), BF),
            pltpu.VMEM((32, R, 128), BF),
            pltpu.VMEM((COLS + 16, 128 * GROUP), BF),
            pltpu.VMEM((EX, 128 * GROUP), BF),
            pltpu.VMEM((COLS + 16, EX), F32),
            pltpu.VMEM((4, CHUNKS, EX, WIDE), BF),
            pltpu.VMEM((4, CHUNKS, EX, WIDE), BF),
            pltpu.VMEM((4 * EX, EX), F32),
            pltpu.VMEM((4, 2 * EX, EX), F32),
            pltpu.VMEM((4, 4 * EX, EX), BF),
            pltpu.VMEM((4, 4 * EX, EX), BF),
            dma((4,)), dma((4,)), dma((4,)), dma((3, 2)), dma((4, 2)), dma((2,)), dma((2,)),
            dma((2, 4)), dma((2, 4)), dma((32,)), dma((32,)), dma((32,)), dma((32,)),
            dma((2, CHUNKS)), dma((2, CHUNKS)), dma((2, CHUNKS)), dma((2, CHUNKS)),
            dma((4, CHUNKS, 2)), dma((4, CHUNKS)), dma((4, 2)), dma((4, 2)),
        ],
        compiler_params=pltpu.CompilerParams(
            collective_id=0, has_side_effects=True, vmem_limit_bytes=60 * 1024 * 1024
        ),
        name="per_example_kernel",
    )(hidden, out_grad, proj_in.T, proj_out.T, owner_ids.reshape(1, TOK), example_ids.reshape(1, TOK))


def solution(mesh):
    in_specs = (
        P("dp", "tensor"),
        P("dp", "tensor"),
        P("tensor", None),
        P("tensor", None),
        P("dp", None),
        P("dp"),
    )
    out_specs = P("tensor", "dp")
    return jax.shard_map(body, mesh=mesh, in_specs=in_specs, out_specs=out_specs, check_vma=False)
```

```python
import jax
import jax.numpy as jnp
from jax import lax
from jax.experimental import pallas as pl
from jax.experimental.pallas import tpu as pltpu
from jax.sharding import PartitionSpec as P

TOK = 1024
PART = 256
EX = 128
R = 64
HALF = 32
COLS = HALF * HALF
GROUP = 4
CHUNKS = 4
WIDE = COLS // CHUNKS
NT = (((1,), (1,)), ((), ()))
MESH = pl.DeviceIdType.MESH
BF = jnp.bfloat16
F32 = jnp.float32


def nt(a, b):
    return lax.dot_general(a, b, NT, preferred_element_type=F32)


def kernel(
    hid, og, pin, pout, own_in, exi_in, out,
    own, exi,
    hbuf, gbuf, pinb, poutb, part_own, rs_send, rs_recv, z_send, z_recv, vals, slots,
    routed, ids_send, ids_recv, sbuf, rbuf, outer, member, acc, bbuf, abuf, keep, sums, c_send, c_recv,
    hsem, gsem, psem, rs_ss, rs_rs, z_ss, z_rs, v_ss, v_rs, i_ss, i_rs, t_ss, t_rs,
    a_ss, a_rs, x_ss, x_rs, b_ss, b_rs, c_ss, c_rs,
):
    dp = lax.axis_index("dp")
    tn = lax.axis_index("tensor")
    y = tn // 2
    zh = lax.rem(tn, 2)
    zl = dp // 8
    x = lax.rem(dp // 2, 4)
    core = lax.rem(dp, 2)

    def remote(src, dst, ss, rs, **where):
        return pltpu.make_async_remote_copy(
            src_ref=src, dst_ref=dst, send_sem=ss, recv_sem=rs,
            device_id=where, device_id_type=MESH,
        )

    def at_y(k):
        return lax.rem(y + k, 4) * 2 + zh

    cp_in = pltpu.make_async_copy(pin, pinb, psem.at[0])
    cp_out = pltpu.make_async_copy(pout, poutb, psem.at[1])
    cp_own = pltpu.make_async_copy(own_in, own, psem.at[2])
    cp_exi = pltpu.make_async_copy(exi_in, exi, psem.at[3])
    cp_own.start()
    cp_exi.start()
    cp_out.start()
    cp_in.start()

    def load(k):
        p = lax.rem(y + 1 + k, 4)
        rows = pl.ds(pl.multiple_of(p * PART, PART), PART)
        return (
            pltpu.make_async_copy(og.at[rows], gbuf.at[p], gsem.at[k]),
            pltpu.make_async_copy(hid.at[rows], hbuf.at[p], hsem.at[k]),
        )

    for k in range(4):
        for cp in load(k):
            cp.start()

    barrier = pltpu.get_barrier_semaphore()

    def greet(k, c):
        pl.semaphore_signal(barrier, inc=1, device_id={"dp": lax.rem(dp + k, 32)}, device_id_type=MESH)
        return c

    lax.fori_loop(1, 32, greet, 0)
    for k in range(1, 4):
        pl.semaphore_signal(barrier, inc=1, device_id={"tensor": at_y(k)}, device_id_type=MESH)
    pl.semaphore_signal(barrier, inc=1, device_id={"tensor": y * 2 + 1 - zh}, device_id_type=MESH)

    def rs_copy(k, ch):
        p = lax.rem(y + 1 + k, 4)
        return remote(
            rs_send.at[k, ch], rs_recv.at[y, ch], rs_ss.at[k, ch], rs_rs.at[y, ch], tensor=p * 2 + zh
        )

    def project(k):
        p = lax.rem(y + 1 + k, 4)
        for cp in load(k):
            cp.wait()
        gp = nt(gbuf[p], poutb[...])
        xp = nt(hbuf[p], pinb[...])
        return jnp.concatenate([xp, gp], 1).T

    cp_out.wait()
    cp_in.wait()
    xc = lax.rem(dp, 8)

    def ids_copy(dz, j):
        zq, xq = lax.rem(zl + dz, 4), lax.rem(xc + j, 8)
        return remote(
            ids_send.at[xq], ids_recv.at[dp], i_ss.at[dz * 8 + j], i_rs.at[dp], dp=zq * 8 + xq
        )

    def ids_start(k, c):
        ids_copy(k // 8, lax.rem(k, 8)).start()
        return c

    for k in range(3):
        both = project(k).astype(BF)
        rs_send[k, 0] = both[:, :128]
        rs_send[k, 1] = both[:, 128:]
        if k == 0:
            pl.semaphore_wait(barrier, 35)
        rs_copy(k, 0).start()
        rs_copy(k, 1).start()
    both = project(3)
    part_own[0] = both[:, :128]
    part_own[1] = both[:, 128:]

    cp_own.wait()
    cp_exi.wait()
    hot = (own[...] - 8 * y == lax.broadcasted_iota(jnp.int32, (8, TOK), 0)).astype(F32)
    tri = (
        lax.broadcasted_iota(jnp.int32, (128, 128), 0) <= lax.broadcasted_iota(jnp.int32, (128, 128), 1)
    ).astype(BF)
    first = (lax.broadcasted_iota(jnp.int32, (8, 128), 0) * 128).astype(F32)
    carry = jnp.zeros((8, 1), F32)
    keys = []
    for b in range(8):
        h = hot[:, 128 * b : 128 * (b + 1)]
        rank = jnp.dot(h.astype(BF), tri, preferred_element_type=F32) + carry
        carry = carry + jnp.sum(h, 1, keepdims=True)
        keys.append(jnp.sum(h * (first + rank), 0, keepdims=True))
    order = [2 * p + ch for ch in range(2) for p in range(4)]
    key = jnp.concatenate([keys[b] for b in order], 1).astype(jnp.int32) - 1
    idrow = (exi[...] + 1).astype(F32)
    idrow = jnp.concatenate([idrow[:, 128 * b : 128 * (b + 1)] for b in order], 1)
    idrow = jnp.broadcast_to(idrow, (16, TOK)).astype(BF)
    for o in range(8):
        hit = key == lax.broadcasted_iota(jnp.int32, (128, TOK), 0) + 128 * o
        slots[128 * o : 128 * (o + 1), :] = hit.astype(F32).astype(BF)
        ids = nt(idrow, slots[128 * o : 128 * (o + 1), :])[0:8, :].astype(BF)
        ids_send[o] = ids
    outer[COLS : COLS + 16, :] = jnp.ones((16, 128 * GROUP), BF)
    acc[...] = jnp.zeros_like(acc)

    def z_copy(ch):
        return remote(z_send.at[ch], z_recv.at[ch], z_ss.at[ch], z_rs.at[ch], tensor=y * 2 + 1 - zh)

    for ch in range(2):
        total = part_own[ch]
        for k in range(1, 4):
            src = lax.rem(y + k, 4)
            remote(
                rs_send.at[0, ch], rs_recv.at[src, ch], rs_ss.at[0, ch], rs_rs.at[src, ch],
                tensor=src * 2 + zh,
            ).wait_recv()
            total = total + rs_recv[src, ch].astype(F32)
        z_send[ch] = total.astype(BF)
        z_copy(ch).start()
        part_own[ch] = total

    lax.fori_loop(1, 32, ids_start, 0)
    ids_recv[dp] = ids_send[xc]

    def v_copy(ch, k):
        return remote(vals.at[ch, y], vals.at[ch, y], v_ss.at[ch, k], v_rs.at[ch, y], tensor=at_y(k))

    for ch in range(2):
        z_copy(ch).wait_recv()
        vals[ch, y] = (part_own[ch] + z_recv[ch].astype(F32)).astype(BF)
        for k in range(1, 4):
            v_copy(ch, k).start()

    for ch in range(2):
        for k in range(1, 4):
            src = lax.rem(y + k, 4)
            remote(
                vals.at[ch, src], vals.at[ch, src], v_ss.at[ch, k], v_rs.at[ch, src], tensor=at_y(k)
            ).wait_recv()
        part = jnp.concatenate([vals[ch, p] for p in range(4)], 1)
        for b in range(2):
            rows = slice(512 * b, 512 * (b + 1))
            placed = nt(part, slots[rows, 512 * ch : 512 * (ch + 1)])
            if ch == 0:
                routed[:, rows] = placed
                continue
            placed = (placed + routed[:, rows]).astype(BF)
            for o in range(4):
                piece = placed[:, 128 * o : 128 * (o + 1)]
                for q in range(4):
                    sbuf[4 * b + o, q, 0:HALF, :] = piece[HALF * (q // 2) : HALF * (q // 2 + 1), :]
                    sbuf[4 * b + o, q, HALF:R, :] = piece[R + HALF * (q % 2) : R + HALF * (q % 2 + 1), :]


    def tok_copy(dz, j):
        zq, xq = lax.rem(zl + dz, 4), lax.rem(xc + j, 8)
        return remote(
            sbuf.at[xq, zq], rbuf.at[dp], t_ss.at[dz * 8 + j], t_rs.at[dp], dp=zq * 8 + xq
        )

    def tok_start(dz):
        def step(j, c):
            tok_copy(dz, j).start()
            return c

        lax.fori_loop(1 if dz == 0 else 0, 8, step, 0)

    for dz in (1, 3, 2, 0):
        tok_start(dz)
    rbuf[dp] = sbuf[xc, zl]

    def kron(g, c):
        half = g // 2
        dz = jnp.where(half < 2, half, 5 - half)
        for s in range(GROUP):
            j = lax.rem(g, 2) * GROUP + s
            src = lax.rem(zl + 4 - dz, 4) * 8 + lax.rem(xc + 8 - j, 8)

            def arrived():
                remote(
                    ids_send.at[0], ids_recv.at[src], i_ss.at[0], i_rs.at[src], dp=src
                ).wait_recv()
                remote(
                    sbuf.at[0, 0], rbuf.at[src], t_ss.at[0], t_rs.at[src], dp=src
                ).wait_recv()

            if s == 0:
                pl.when(g > 0)(arrived)
            else:
                arrived()
            xr = rbuf[src, 0:HALF, :].astype(F32)
            gr = rbuf[src, HALF:R, :].astype(F32)
            lanes = slice(128 * s, 128 * (s + 1))
            for i in range(HALF):
                outer[HALF * i : HALF * (i + 1), lanes] = (xr[i : i + 1, :] * gr).astype(BF)
            ids = ids_recv[src].astype(F32)[0:1, :].astype(jnp.int32)
            member[:, lanes] = (
                (ids == lax.broadcasted_iota(jnp.int32, (EX, 128), 0) + 1).astype(F32).astype(BF)
            )
        acc[...] += nt(outer[...], member[...])
        return c

    lax.fori_loop(0, 32 // GROUP, kron, 0)

    yp, ym = at_y(1), at_y(3)
    before, after, across = lax.rem(y + 3, 4), lax.rem(y + 1, 4), lax.rem(y + 2, 4)
    r = lax.rem(x + 4 - 2 * zh, 4)
    mine = jnp.where(r < 2, r, 3 - r)
    other = 1 - mine
    twin = dp + 1 - 2 * core

    def at_x(k):
        return zl * 8 + lax.rem(x + k, 4) * 2 + core

    def b_copy(q, n, way):
        return remote(
            bbuf.at[q, n], bbuf.at[q, n], b_ss.at[q, n, way], b_rs.at[q, n], tensor=yp if way == 0 else ym
        )

    def b_wait(q, n):
        b_copy(q, n, 0).wait_recv()

    def a_first(n, side):
        return remote(
            bbuf.at[y, n], abuf.at[mine * 2 + core, n], a_ss.at[side, n], a_rs.at[mine, n],
            dp=at_x(1 if side == 0 else 3),
        )

    def a_next(n):
        slot = abuf.at[mine * 2 + core, n]
        return remote(slot, slot, a_ss.at[0, n], a_rs.at[mine, n], dp=at_x(1 + 2 * (r - 2)))

    def a_wait(which, n):
        slot = abuf.at[which * 2 + core, n]
        remote(slot, slot, a_ss.at[0, n], a_rs.at[which, n], dp=at_x(1)).wait_recv()

    def x_copy(which, n):
        slot = abuf.at[which * 2 + core, n]
        return remote(slot, slot, x_ss.at[which, n], x_rs.at[which, n], dp=twin)

    def x_wait(which, n):
        slot = abuf.at[which * 2 + 1 - core, n]
        remote(slot, slot, x_ss.at[which, n], x_rs.at[which, n], dp=twin).wait_recv()

    scale = 1.0 / jnp.maximum(acc[COLS : COLS + 1, :], 1.0)
    for n in range(CHUNKS):
        piece = (acc[WIDE * n : WIDE * (n + 1), :] * scale).T.astype(BF)
        bbuf[y, n] = piece

        @pl.when(r < 2)
        def _():
            a_first(n, 0).start()
            a_first(n, 1).start()
            abuf[mine * 2 + core, n] = piece
            x_copy(mine, n).start()

        b_copy(y, n, 0).start()
        b_copy(y, n, 1).start()

    def c_copy(q, which):
        rows = pl.ds(pl.multiple_of(2 * EX * which, 2 * EX), 2 * EX)
        return remote(
            c_send.at[q, rows], c_recv.at[zl, rows], c_ss.at[q, which], c_rs.at[zl, which],
            dp=q * 8 + x * 2 + core,
        )

    def term(which, q, n):
        return nt(abuf[pl.ds(which * 2, 2), n].reshape(2 * EX, WIDE), bbuf[q, n])

    def block(which, q, product=None, begin=0):
        rows = pl.ds(pl.multiple_of(2 * EX * which, 2 * EX), 2 * EX)
        for n in range(begin, CHUNKS):
            product = term(which, q, n) if product is None else product + term(which, q, n)
        product = product * (1.0 / R)

        @pl.when(q == zl)
        def _():
            keep[rows, :] = product

        @pl.when(q != zl)
        def _():
            c_send[q, rows, :] = product.astype(BF)
            c_copy(q, which).start()

    @pl.when(r < 2)
    def _():
        for n in range(CHUNKS):
            x_wait(mine, n)
        block(mine, y)

    for n in range(CHUNKS):
        @pl.when(r >= 2)
        def _():
            for m in ((0, 1, 2, 3), (), (), ())[n]:
                a_wait(mine, m)
                a_next(m).start()
                x_copy(mine, m).start()

        b_wait(before, n)
        if n < CHUNKS // 2:
            b_copy(before, n, 0).start()
        b_wait(after, n)
        if n >= CHUNKS // 2:
            b_copy(after, n, 1).start()

    @pl.when(r >= 2)
    def _():
        for n in range(CHUNKS):
            x_wait(mine, n)
        block(mine, y)

    block(mine, after)
    block(mine, before)
    near = (y, after, before)
    for n in range(CHUNKS):
        a_wait(other, n)
        x_copy(other, n).start()
        if n > 0:
            x_wait(other, n - 1)
            for t in range(3):
                new = term(other, near[t], n - 1)
                sums[near[t]] = new if n == 1 else sums[near[t]] + new
    for n in range(CHUNKS):
        b_wait(across, n)
    block(mine, across)
    partial = term(other, across, 0)
    for n in range(1, CHUNKS - 1):
        partial = partial + term(other, across, n)
    sums[across] = partial
    x_wait(other, CHUNKS - 1)
    for k in (2, 1, 3, 0):
        q = lax.rem(zl + k, 4)
        block(other, q, sums[q], CHUNKS - 1)

    for which in range(2):
        rows = slice(2 * EX * which, 2 * EX * (which + 1))
        result = keep[rows, :]
        for k in range(1, 4):
            src = lax.rem(zl + k, 4)
            remote(
                c_send.at[src, rows], c_recv.at[src, rows], c_ss.at[src, which], c_rs.at[src, which],
                dp=src * 8 + x * 2 + core,
            ).wait_recv()
            result = result + c_recv[src, rows, :].astype(F32)
        out[rows, :] = result

    def left(k, c):
        tok_copy(k // 8, lax.rem(k, 8)).wait_send()
        ids_copy(k // 8, lax.rem(k, 8)).wait_send()
        return c

    lax.fori_loop(1, 32, left, 0)
    for k in range(3):
        rs_copy(k, 0).wait_send()
        rs_copy(k, 1).wait_send()
        for h in range(2):
            v_copy(h, k + 1).wait_send()
            c_copy(lax.rem(zl + k + 1, 4), h).wait_send()
    for h in range(2):
        z_copy(h).wait_send()
    for n in range(CHUNKS):
        b_copy(y, n, 0).wait_send()
        b_copy(y, n, 1).wait_send()
        if n < CHUNKS // 2:
            b_copy(before, n, 0).wait_send()
        else:
            b_copy(after, n, 1).wait_send()
        x_copy(0, n).wait_send()
        x_copy(1, n).wait_send()

        @pl.when(r < 2)
        def _():
            a_first(n, 0).wait_send()
            a_first(n, 1).wait_send()

        @pl.when(r >= 2)
        def _():
            a_next(n).wait_send()


def body(hidden, out_grad, proj_in, proj_out, owner_ids, example_ids):
    wide, model = hidden.shape[1], out_grad.shape[1]
    hbm = pl.BlockSpec(memory_space=pltpu.HBM)
    vmem = pl.BlockSpec(memory_space=pltpu.VMEM)
    dma = pltpu.SemaphoreType.DMA
    return pl.pallas_call(
        kernel,
        out_shape=jax.ShapeDtypeStruct((4 * EX, EX), F32),
        in_specs=[hbm] * 6,
        out_specs=vmem,
        scratch_shapes=[
            pltpu.VMEM((1, TOK), jnp.int32),
            pltpu.VMEM((1, TOK), jnp.int32),
            pltpu.VMEM((4, PART, wide), BF),
            pltpu.VMEM((4, PART, model), BF),
            pltpu.VMEM((R, wide), BF),
            pltpu.VMEM((R, model), BF),
            pltpu.VMEM((2, 2 * R, 128), F32),
            pltpu.VMEM((3, 2, 2 * R, 128), BF),
            pltpu.VMEM((4, 2, 2 * R, 128), BF),
            pltpu.VMEM((2, 2 * R, 128), BF),
            pltpu.VMEM((2, 2 * R, 128), BF),
            pltpu.VMEM((2, 4, 2 * R, 128), BF),
            pltpu.VMEM((8 * 128, TOK), BF),
            pltpu.VMEM((2 * R, 8 * 128), F32),
            pltpu.VMEM((8, 8, 128), BF),
            pltpu.VMEM((32, 8, 128), BF),
            pltpu.VMEM((8, 4, R, 128), BF),
            pltpu.VMEM((32, R, 128), BF),
            pltpu.VMEM((COLS + 16, 128 * GROUP), BF),
            pltpu.VMEM((EX, 128 * GROUP), BF),
            pltpu.VMEM((COLS + 16, EX), F32),
            pltpu.VMEM((4, CHUNKS, EX, WIDE), BF),
            pltpu.VMEM((4, CHUNKS, EX, WIDE), BF),
            pltpu.VMEM((4 * EX, EX), F32),
            pltpu.VMEM((4, 2 * EX, EX), F32),
            pltpu.VMEM((4, 4 * EX, EX), BF),
            pltpu.VMEM((4, 4 * EX, EX), BF),
            dma((4,)), dma((4,)), dma((4,)), dma((3, 2)), dma((4, 2)), dma((2,)), dma((2,)),
            dma((2, 4)), dma((2, 4)), dma((32,)), dma((32,)), dma((32,)), dma((32,)),
            dma((2, CHUNKS)), dma((2, CHUNKS)), dma((2, CHUNKS)), dma((2, CHUNKS)),
            dma((4, CHUNKS, 2)), dma((4, CHUNKS)), dma((4, 2)), dma((4, 2)),
        ],
        compiler_params=pltpu.CompilerParams(
            collective_id=0, has_side_effects=True, vmem_limit_bytes=60 * 1024 * 1024
        ),
        name="per_example_kernel",
    )(hidden, out_grad, proj_in.T, proj_out.T, owner_ids.reshape(1, TOK), example_ids.reshape(1, TOK))


def solution(mesh):
    in_specs = (
        P("dp", "tensor"),
        P("dp", "tensor"),
        P("tensor", None),
        P("tensor", None),
        P("dp", None),
        P("dp"),
    )
    out_specs = P("tensor", "dp")
    return jax.shard_map(body, mesh=mesh, in_specs=in_specs, out_specs=out_specs, check_vma=False)
```
